128 devices in a mesh: dp: 32 (over z, y, x_hi), section: 2 (over core), chan: 2 (over x_lo).
Axes of the slice: x: 4 (x_hi: 2, x_lo: 2; x = x_hi * 2 + x_lo), y: 4, z: 4, core: 2. Of those that a mesh axis runs over, the one named last changes fastest.
Arguments:
- clips: bfloat16 [32, 512, 4, 128], P('dp', 'chan'), may hold values from -24 to 24
- conv_weight: bfloat16 [2, 27, 512, 512], P('section', None, 'chan'), may hold values from -0.0546875 to 0.0546875
- norm_gain: float32 [2, 512], P('section', 'chan'), may hold values from 0.1 to 1.9
- norm_bias: float32 [2, 512], P('section', 'chan'), may hold values from -3 to 3
- cotangent: bfloat16 [32, 512, 4, 128], P('dp', 'chan'), may hold values from -0.046875 to 0.046875
Outputs:
- weight_grad: float32 [2, 27, 512, 512], P('section', None, 'chan')
- gain_grad: float32 [2, 512], P('section', 'chan')
- bias_grad: float32 [2, 512], P('section', 'chan')
The draws below stay inside these ranges and needn't reach their ends.
All inputs are finite; a program needn't handle non-finite values.
Results may differ from the reference program's by a relative error of at most 0.006.
Values may be sent and summed in bfloat16 or wider, within the bound.
A program may use at most 128 MiB of HBM per device.

```python
import jax
import jax.numpy as jnp
from jax import lax

C = 512
GROUPS = 32
HT = 8
WD = 16
FRAMES = 4
PIX = 128
CLIPS = 32
LAYERS = 2
N_CHAN = 2


def draw_clips(key, part):
    subkeys = jax.random.split(key, 3)
    base_draw = jax.random.truncated_normal(subkeys[0], -4.0, 4.0, (CLIPS, C, FRAMES, PIX), jnp.float32)
    channel_scale = jnp.exp(jax.random.uniform(subkeys[1], (CLIPS, C, 1, 1), jnp.float32, -0.8, 0.8))
    pixel_scale = jnp.exp(jax.random.uniform(subkeys[2], (CLIPS, 1, FRAMES, PIX), jnp.float32, -0.8, 0.8))
    values = base_draw * channel_scale * pixel_scale
    return values.astype(jnp.bfloat16)


def level_of(rng, dims, cuts, least, top_value):
    def one(axis_at, blocks):
        steps = jax.random.uniform(jax.random.fold_in(jax.random.fold_in(rng, 6), axis_at), (blocks,), jnp.float32, least / len(cuts), top_value / len(cuts))
        return jnp.repeat(jnp.exp(steps), dims[axis_at] // blocks).reshape((-1,) + (1,) * (len(dims) - axis_at - 1))

    loudness = one(*cuts[0])
    for cut in cuts[1:]:
        loudness = loudness * one(*cut)
    return loudness


def normal_values(own_key, extent, deviation, most, cuts=(), held_as=jnp.bfloat16):
    values = deviation * jax.random.normal(own_key, extent, jnp.float32)
    if cuts:
        values = values * level_of(own_key, extent, cuts, -0.22, 0.18)
    return jnp.clip(values, -most, most).astype(held_as)


def setup_inputs(seed: int = 0) -> dict:
    seeds = jax.random.split(jax.random.key(seed), 6)
    return {
        "clips": draw_clips(jax.random.fold_in(seeds[5], 71), 0),
        "conv_weight": normal_values(seeds[1], (LAYERS, 27, C, C), (27 * C) ** -0.5, 0.0546875, ((0, 2), (2, 2))),
        "norm_gain": jnp.clip(1.0 + 0.18 * jax.random.normal(seeds[2], (LAYERS, C), jnp.float32), 0.1, 1.9),
        "norm_bias": normal_values(seeds[3], (LAYERS, C), 0.5, 3.0, ((0, 2), (1, 2)), jnp.float32),
        "cotangent": normal_values(seeds[4], (CLIPS, C, FRAMES, PIX), (CLIPS * FRAMES * PIX) ** -0.5, 0.046875, ((0, 32), (1, 2))),
    }


EPSILON = 1e-05

def norm_parts(act_block, gain_row, bias_row, group_count):
    channels, frames, pixels = act_block.shape
    values = act_block.astype(jnp.float32).reshape(group_count, channels // group_count, frames, pixels)
    centre = lax.optimization_barrier(jnp.mean(values, axis=(1, 3), keepdims=True))
    spread = lax.optimization_barrier(jnp.mean(jnp.square(values - centre), axis=(1, 3), keepdims=True))
    inv_std = lax.rsqrt(spread + EPSILON)
    normed = ((values - centre) * inv_std).reshape(channels, frames, pixels)
    shifted = normed * gain_row[:, None, None] + bias_row[:, None, None]
    return (normed, shifted, inv_std)

def norm_backward(grad_hidden, normed, shifted, inv_std, gain_row, group_count):
    channels, frames, pixels = normed.shape
    sigmoid_part = jax.nn.sigmoid(shifted)
    grad_shift = grad_hidden * sigmoid_part * (1.0 + shifted * (1.0 - sigmoid_part))
    gain_term = lax.optimization_barrier(jnp.sum(grad_shift * normed, axis=(1, 2)))
    bias_term = lax.optimization_barrier(jnp.sum(grad_shift, axis=(1, 2)))
    grad_normed = (grad_shift * gain_row[:, None, None]).reshape(group_count, channels // group_count, frames, pixels)
    grouped = normed.reshape(group_count, channels // group_count, frames, pixels)
    mean_grad = lax.optimization_barrier(jnp.mean(grad_normed, axis=(1, 3), keepdims=True))
    mean_cross = lax.optimization_barrier(jnp.mean(grad_normed * grouped, axis=(1, 3), keepdims=True))
    grad_act = ((grad_normed - mean_grad - grouped * mean_cross) * inv_std).reshape(channels, frames, pixels)
    return (grad_act, gain_term, bias_term)

def tap_stack(extended, height, grid_width):
    channels, span_frames, pixels = extended.shape
    frames = span_frames - 2
    lattice = extended.reshape(channels, span_frames, height, grid_width)
    lattice = jnp.pad(lattice, ((0, 0), (0, 0), (1, 1), (1, 1)))
    tap_list = []
    for tap_time in range(3):
        for tap_row in range(3):
            for tap_col in range(3):
                tap_list.append(lattice[:, tap_time:tap_time + frames, tap_row:tap_row + height, tap_col:tap_col + grid_width])
    stacked = jnp.stack(tap_list, axis=0)
    return stacked.reshape(27 * channels, frames * height * grid_width)

def tap_scatter(grads, channels, frames, height, grid_width):
    tap_grads = grads.reshape(27, channels, frames, height, grid_width)
    padded = jnp.zeros((channels, frames + 2, height + 2, grid_width + 2), jnp.float32)
    tap_index = 0
    for tap_time in range(3):
        for tap_row in range(3):
            for tap_col in range(3):
                padded = padded.at[:, tap_time:tap_time + frames, tap_row:tap_row + height, tap_col:tap_col + grid_width].add(tap_grads[tap_index])
                tap_index += 1
    return padded[:, :, 1:-1, 1:-1].reshape(channels, frames + 2, height * grid_width)

def reference(clips, conv_weight, norm_gain, norm_bias, cotangent):
    shard_width = C // N_CHAN
    row_count = FRAMES * PIX

    def one_clip(totals, inputs_pair):
        grad_weight, grad_gain, grad_bias = totals
        clip_acts, upstream = inputs_pair
        saved_acts = []
        act_now = clip_acts
        for layer_index in range(LAYERS):
            saved_acts.append(act_now)
            normed, shifted, inv_std = norm_parts(act_now, norm_gain[layer_index], norm_bias[layer_index], GROUPS)
            hidden = (shifted * jax.nn.sigmoid(shifted)).astype(jnp.bfloat16)
            extended = jnp.concatenate([jnp.zeros((C, 2, PIX), jnp.bfloat16), hidden], axis=1)
            tap_major = tap_stack(extended, HT, WD).reshape(27, C, row_count)
            summed_conv = jnp.zeros((C, row_count), jnp.float32)
            for member in range(N_CHAN):
                inputs_part = tap_major[:, member * shard_width:(member + 1) * shard_width].reshape(27 * shard_width, row_count)
                weight_part = conv_weight[layer_index][:, member * shard_width:(member + 1) * shard_width].reshape(27 * shard_width, C)
                partial_value = lax.dot_general(weight_part, inputs_part, (((0,), (0,)), ((), ())), preferred_element_type=jnp.float32)
                rounded = lax.optimization_barrier(partial_value.astype(jnp.bfloat16))
                summed_conv = summed_conv + rounded.astype(jnp.float32)
            act_now = (act_now.astype(jnp.float32) + summed_conv.reshape(C, FRAMES, PIX)).astype(jnp.bfloat16)
        for layer_index in reversed(range(LAYERS)):
            act_now = saved_acts[layer_index]
            gain_row = norm_gain[layer_index]
            normed, shifted, inv_std = norm_parts(act_now, gain_row, norm_bias[layer_index], GROUPS)
            hidden = (shifted * jax.nn.sigmoid(shifted)).astype(jnp.bfloat16)
            extended = jnp.concatenate([jnp.zeros((C, 2, PIX), jnp.bfloat16), hidden], axis=1)
            stacked = tap_stack(extended, HT, WD)
            flat_up = upstream.reshape(C, row_count)
            weight_flat = conv_weight[layer_index].reshape(27 * C, C)
            weight_term = lax.dot_general(stacked, flat_up, (((1,), (1,)), ((), ())), preferred_element_type=jnp.float32)
            grad_weight = grad_weight.at[layer_index].add(weight_term.reshape(27, C, C))
            grad_stack = jnp.dot(weight_flat, flat_up, preferred_element_type=jnp.float32)
            grad_ext = tap_scatter(grad_stack, C, FRAMES, HT, WD)
            grad_act, gain_term, bias_term = norm_backward(grad_ext[:, 2:], normed, shifted, inv_std, gain_row, GROUPS)
            grad_gain = grad_gain.at[layer_index].add(gain_term)
            grad_bias = grad_bias.at[layer_index].add(bias_term)
            upstream = (upstream.astype(jnp.float32) + grad_act).astype(jnp.bfloat16)
        return ((grad_weight, grad_gain, grad_bias), None)
    start_totals = (jnp.zeros((LAYERS, 27, C, C), jnp.float32), jnp.zeros((LAYERS, C), jnp.float32), jnp.zeros((LAYERS, C), jnp.float32))
    totals, unused_out = lax.scan(one_clip, start_totals, (clips, cotangent))
    return (totals[0], totals[1], totals[2])
```

```python
import jax
import jax.numpy as jnp
from jax import lax
from jax.experimental import pallas as pl
from jax.experimental.pallas import tpu as pltpu
from jax.sharding import PartitionSpec as P

EPSILON = 1e-05
MESH = pl.DeviceIdType.MESH
BF = jnp.bfloat16
F32 = jnp.float32

CH = 256
FULL = 512
POS = 512
SLICE = 128
GROUP = 16
UNITS = 432
BLK = UNITS // 4
HALF = BLK // 2


def coords():
    dp = lax.axis_index("dp")
    return dp // 8, dp // 2 % 4, dp % 2, lax.axis_index("section"), lax.axis_index("chan")


def remote(src, dst, send_sem, recv_sem, dp, section, chan):
    return pltpu.make_async_remote_copy(
        src_ref=src,
        dst_ref=dst,
        send_sem=send_sem,
        recv_sem=recv_sem,
        device_id={"dp": dp, "section": section, "chan": chan},
        device_id_type=MESH,
    )


def norm_frame(values):
    scale = 1.0 / (GROUP * 128)
    centre = jnp.sum(values, axis=(1, 2), keepdims=True) * scale
    moved = values - centre
    spread = jnp.sum(moved * moved, axis=(1, 2), keepdims=True) * scale
    inv_std = lax.rsqrt(spread + EPSILON)
    return moved * inv_std, inv_std


def norm_forward(act, gain, bias):
    grouped = act.reshape(GROUP, GROUP, POS)
    parts = [norm_frame(grouped[:, :, 128 * f : 128 * f + 128]) for f in range(4)]
    normed = jnp.concatenate([p[0] for p in parts], axis=2)
    return normed, normed * gain + bias, [p[1] for p in parts]


def silu(shifted):
    return shifted * (1.0 / (1.0 + jnp.exp(-shifted)))


def norm_backward(grad_hidden, normed, shifted, inv_std, gain):
    sig = 1.0 / (1.0 + jnp.exp(-shifted))
    grad_shift = grad_hidden.reshape(GROUP, GROUP, POS) * sig * (1.0 + shifted * (1.0 - sig))
    gain_term = jnp.sum(grad_shift * normed, axis=2, keepdims=True)
    bias_term = jnp.sum(grad_shift, axis=2, keepdims=True)
    return grad_shift * gain, gain_term, bias_term


def norm_input_grad(grad_normed, normed, inv_std):
    scale = 1.0 / (GROUP * 128)
    parts = []
    for f in range(4):
        g, n = grad_normed[:, :, 128 * f : 128 * f + 128], normed[:, :, 128 * f : 128 * f + 128]
        mean_grad = jnp.sum(g, axis=(1, 2), keepdims=True) * scale
        mean_cross = jnp.sum(g * n, axis=(1, 2), keepdims=True) * scale
        parts.append((g - mean_grad - n * mean_cross) * inv_std[f])
    return jnp.concatenate(parts, axis=2)


def small_rows(gain_term, bias_term):
    lane = lax.broadcasted_iota(jnp.int32, (CH, 128), 1)
    gain_col = jnp.broadcast_to(gain_term.reshape(CH, 1), (CH, 128))
    bias_col = jnp.broadcast_to(bias_term.reshape(CH, 1), (CH, 128))
    both = jnp.where(lane == 0, gain_col, jnp.where(lane == 1, bias_col, 0.0))
    return both.T[:8]


def shifted_columns(values, store):
    col = lax.broadcasted_iota(jnp.int32, values.shape, 0) % 16
    store(0, jnp.where(col == 0, 0.0, pltpu.roll(values, 1, 0)))
    store(1, values)
    store(2, jnp.where(col == 15, 0.0, pltpu.roll(values, POS - 1, 0)))


def conv_forward(lattice, weights, acc, wait_weights):
    for t in (2, 1, 0):
        wait_weights(t)
        rows = 128 * (t + 2)

        def tap_row(r, carry, t=t, rows=rows):
            lhs = lattice[0 : t + 2, pl.ds(r, 8), :, 0 : 3 * CH].reshape(rows, 3 * CH)
            rhs = weights[pl.ds(9 * t + 3 * r, 3)].reshape(3 * CH, FULL)
            part = jnp.dot(lhs, rhs, preferred_element_type=F32)
            acc[pl.ds(128 * (2 - t), rows)] = acc[pl.ds(128 * (2 - t), rows)] + part
            return carry

        lax.fori_loop(0, 3, tap_row, 0)


def conv_transposed(lattice, weights, acc, wait_weights):
    for t in (2, 1, 0):
        wait_weights(t)
        cols = 128 * (t + 2)

        def tap_row(r, carry, t=t, cols=cols):
            part = None
            for v in range(3):
                rhs = lattice[2 - t : 4, pl.ds(2 - r, 8), :, v * FULL : (v + 1) * FULL].reshape(cols, FULL)
                one = lax.dot_general(
                    weights[9 * t + 3 * r + 2 - v], rhs, (((1,), (1,)), ((), ())), preferred_element_type=F32
                )
                part = one if part is None else part + one
            acc[:, 0:cols] = acc[:, 0:cols] + part
            return carry

        lax.fori_loop(0, 3, tap_row, 0)


def weight_gradient(hidden_all, lattice, out):
    for t in (2, 1, 0):
        cols = 128 * (t + 2)
        lhs = jnp.concatenate([hidden_all[:, POS * k : POS * k + cols] for k in range(4)], axis=1)

        def tap_row(r, carry, t=t, cols=cols, lhs=lhs):
            rhs = lattice[:, 2 - t : 4, pl.ds(2 - r, 8)].reshape(4 * cols, 3 * SLICE)
            part = jnp.dot(lhs, rhs, preferred_element_type=F32).astype(BF)
            for v in range(3):
                tap = 9 * t + 3 * r + 2 - v
                out[pl.ds(16 * tap, 16)] = part[:, v * SLICE : (v + 1) * SLICE].reshape(16, 16, SLICE)
            return carry

        lax.fori_loop(0, 3, tap_row, 0)


def front_kernel(
    clips_ref, cot_ref, gain_ref, bias_ref, w_hbm, d_ref, small_ref,
    weights, lattice, slice_lattice, hidden_own, hidden_all, adj_own, full, slices, conv_out, conv_in, acc_y, acc_g, normed_s, inv_s,
    w_sems, own_sems, full_send, full_recv, slice_send, slice_recv, hid_send, hid_recv, y_send, y_recv,
):
    z, y, x, section, chan = coords()
    here = z * 8 + y * 2 + x

    def at_z(k):
        return k * 8 + y * 2 + x

    def at_y(k):
        return z * 8 + k * 2 + x

    barrier = pltpu.get_barrier_semaphore()

    def greet(dp, s, c):
        pl.semaphore_signal(barrier, inc=1, device_id={"dp": dp, "section": s, "chan": c}, device_id_type=MESH)

    for s in (0, 1):
        for c in (0, 1):
            for step in (1, 2, 3):
                greet(at_z((z + step) % 4), s, c)
                greet(at_y((y + step) % 4), s, c)
    greet(here, 1 - section, chan)
    greet(here, section, 1 - chan)
    greet(here, 1 - section, 1 - chan)
    pl.semaphore_wait(barrier, 27)

    def w_copy(t):
        return pltpu.make_async_copy(w_hbm.at[pl.ds(9 * t, 9)], weights.at[pl.ds(9 * t, 9)], w_sems.at[t])

    for t in (2, 1, 0):
        w_copy(t).start()

    def wait_weights(t):
        w_copy(t).wait()

    gain = gain_ref[...].reshape(GROUP, GROUP, 1)
    bias = bias_ref[...].reshape(GROUP, GROUP, 1)

    group = section * y + (1 - section) * z

    def ring(k):
        return section * at_y(k) + (1 - section) * at_z(k)

    def hidden_copy(step):
        return remote(
            hidden_own, hidden_all.at[:, pl.ds(pl.multiple_of(group * POS, POS), POS)],
            hid_send.at[step - 1], hid_recv.at[(4 - step) % 4], ring((group + step) % 4), section, chan,
        )

    def hidden_own_copy():
        return pltpu.make_async_copy(
            hidden_own, hidden_all.at[:, pl.ds(pl.multiple_of(group * POS, POS), POS)], own_sems.at[0]
        )

    def full_copy(c):
        return remote(adj_own, full.at[chan], full_send.at[c], full_recv.at[chan], here, 0, c)

    def cot_full_copy():
        return remote(adj_own, full.at[chan], full_send.at[0], full_recv.at[chan], here, 1, 1 - chan)

    def slice_copy(jj, c, dest_section):
        j = 2 * chan + jj
        slot = dest_section * y + (1 - dest_section) * z
        dp = dest_section * at_y(j) + (1 - dest_section) * at_z(j)
        return remote(
            adj_own.at[:, pl.ds(SLICE * jj, SLICE)], slices.at[slot], slice_send.at[2 * jj + c],
            slice_recv.at[slot], dp, dest_section, c,
        )

    def own_slice_copy():
        return pltpu.make_async_copy(
            adj_own.at[:, pl.ds(pl.multiple_of(y % 2 * SLICE, SLICE), SLICE)], slices.at[y], own_sems.at[1]
        )

    def conv_copy(c):
        return remote(conv_out.at[c], conv_in.at[chan], y_send.at[c], y_recv.at[chan], here, 1, c)

    zero_row = jnp.zeros((4, 1, 16, 3 * FULL), BF)
    lattice[:, 0:1] = zero_row
    lattice[:, 9:10] = zero_row
    zero_slice = jnp.zeros((4, 4, 1, 16, 3 * SLICE), BF)
    slice_lattice[:, :, 0:1] = zero_slice
    slice_lattice[:, :, 9:10] = zero_slice

    def fill_full(which, width, values):
        def store(v, moved):
            start = v * width + which
            lattice[:, 1:9, :, start : start + CH] = moved.astype(BF).reshape(4, 8, 16, CH)

        shifted_columns(values, store)

    @pl.when(section == 0)
    def _():
        act = clips_ref[...].astype(F32)
        normed, shifted, inv_std = norm_forward(act, gain, bias)
        hidden = silu(shifted).astype(BF).reshape(CH, POS)
        hidden_own[...] = hidden
        for step in (1, 2, 3):
            hidden_copy(step).start()
        hidden_own_copy().start()
        normed_s[...] = normed
        for f in range(4):
            inv_s[f] = jnp.broadcast_to(inv_std[f], (GROUP, 1, 128))
        fill_full(0, CH, hidden.astype(F32).T)
        acc_y[...] = jnp.zeros_like(acc_y)
        conv_forward(lattice, weights, acc_y, wait_weights)
        for c in range(2):
            conv_out[c] = acc_y[:, c * CH : (c + 1) * CH].astype(BF)
            conv_copy(c).start()

    @pl.when(section == 1)
    def _():
        own = cot_ref[...].astype(F32).T
        adj_own[...] = own.astype(BF)
        cot_full_copy().start()
        for jj in range(2):
            for c in range(2):

                @pl.when((2 * chan + jj != y) | (chan != c))
                def _(jj=jj, c=c):
                    slice_copy(jj, c, 1).start()

        @pl.when(y // 2 == chan)
        def _():
            own_slice_copy().start()

        full[chan] = own.astype(BF)
        remote(adj_own, full.at[1 - chan], full_send.at[0], full_recv.at[1 - chan], here, 1, 1 - chan).wait_recv()
        for c in range(2):
            fill_full(c * CH, FULL, full[c].astype(F32))
        acc_g[...] = jnp.zeros_like(acc_g)
        conv_transposed(lattice, weights, acc_g, wait_weights)
        for c in range(2):
            remote(conv_out.at[c], conv_in.at[c], y_send.at[c], y_recv.at[c], here, 1, c).wait_recv()
        summed = conv_in[0].astype(F32) + conv_in[1].astype(F32)
        act = (clips_ref[...].astype(F32) + summed.T).astype(BF).astype(F32)
        normed, shifted, inv_std = norm_forward(act, gain, bias)
        hidden_own[...] = silu(shifted).astype(BF).reshape(CH, POS)
        for step in (1, 2, 3):
            hidden_copy(step).start()
        hidden_own_copy().start()
        grad_normed, gain_term, bias_term = norm_backward(acc_g[...], normed, shifted, inv_std, gain)
        small_ref[...] = small_rows(gain_term, bias_term)
        grad_act = norm_input_grad(grad_normed, normed, inv_std).reshape(CH, POS)
        adjoint = (cot_ref[...].astype(F32) + grad_act).T.astype(BF)
        cot_full_copy().wait_send()
        for jj in range(2):
            for c in range(2):

                @pl.when((2 * chan + jj != y) | (chan != c))
                def _(jj=jj, c=c):
                    slice_copy(jj, c, 1).wait_send()

        @pl.when(y // 2 == chan)
        def _():
            own_slice_copy().wait()

        adj_own[...] = adjoint
        for jj in range(2):
            for c in range(2):
                slice_copy(jj, c, 0).start()
        for c in range(2):
            full_copy(c).start()
        for k in range(4):

            @pl.when((k != y) | (y // 2 != chan))
            def _(k=k):
                remote(
                    adj_own.at[:, pl.ds(0, SLICE)], slices.at[k], slice_send.at[0], slice_recv.at[k], here, 1, 1 - chan
                ).wait_recv()

    @pl.when(section == 0)
    def _():
        for k in range(4):
            remote(
                adj_own.at[:, pl.ds(0, SLICE)], slices.at[k], slice_send.at[0], slice_recv.at[k], here, 1, chan
            ).wait_recv()

    for k in range(4):

        def store(v, moved, k=k):
            slice_lattice[k, :, 1:9, :, v * SLICE : (v + 1) * SLICE] = moved.astype(BF).reshape(4, 8, 16, SLICE)

        shifted_columns(slices[k].astype(F32), store)
    hidden_own_copy().wait()
    for step in (1, 2, 3):
        came = (group + step) % 4
        remote(
            hidden_own, hidden_all.at[:, pl.ds(pl.multiple_of(came * POS, POS), POS)],
            hid_send.at[step - 1], hid_recv.at[step], ring((group + step) % 4), section, chan,
        ).wait_recv()
    weight_gradient(hidden_all, slice_lattice, d_ref)

    @pl.when(section == 0)
    def _():
        for c in range(2):
            remote(adj_own, full.at[c], full_send.at[c], full_recv.at[c], here, 1, chan).wait_recv()
            fill_full(c * CH, FULL, full[c].astype(F32))
        acc_g[...] = jnp.zeros_like(acc_g)
        conv_transposed(lattice, weights, acc_g, lambda t: None)
        normed = normed_s[...]
        shifted = normed * gain + bias
        inv_std = [inv_s[f] for f in range(4)]
        unused, gain_term, bias_term = norm_backward(acc_g[...], normed, shifted, inv_std, gain)
        small_ref[...] = small_rows(gain_term, bias_term)
        for c in range(2):
            conv_copy(c).wait_send()

    @pl.when(section == 1)
    def _():
        for jj in range(2):
            for c in range(2):
                slice_copy(jj, c, 0).wait_send()
        for c in range(2):
            full_copy(c).wait_send()

    for step in (1, 2, 3):
        hidden_copy(step).wait_send()


def front(clips, cot, gain, bias, weights):
    vmem = pl.BlockSpec(memory_space=pltpu.VMEM)
    dma = pltpu.SemaphoreType.DMA
    return pl.pallas_call(
        front_kernel,
        out_shape=(jax.ShapeDtypeStruct((UNITS, 16, SLICE), BF), jax.ShapeDtypeStruct((8, CH), F32)),
        in_specs=[vmem, vmem, vmem, vmem, pl.BlockSpec(memory_space=pl.ANY)],
        out_specs=(vmem, vmem),
        scratch_shapes=[
            pltpu.VMEM((27, CH, FULL), BF),
            pltpu.VMEM((4, 10, 16, 3 * FULL), BF),
            pltpu.VMEM((4, 4, 10, 16, 3 * SLICE), BF),
            pltpu.VMEM((CH, POS), BF),
            pltpu.VMEM((CH, 4 * POS), BF),
            pltpu.VMEM((POS, CH), BF),
            pltpu.VMEM((2, POS, CH), BF),
            pltpu.VMEM((4, POS, SLICE), BF),
            pltpu.VMEM((2, POS, CH), BF),
            pltpu.VMEM((2, POS, CH), BF),
            pltpu.VMEM((POS, FULL), F32),
            pltpu.VMEM((CH, POS), F32),
            pltpu.VMEM((GROUP, GROUP, POS), F32),
            pltpu.VMEM((4, GROUP, 1, 128), F32),
            dma((3,)), dma((2,)), dma((2,)), dma((2,)), dma((4,)), dma((4,)), dma((3,)), dma((4,)), dma((2,)), dma((2,)),
        ],
        compiler_params=pltpu.CompilerParams(collective_id=1, has_side_effects=True, vmem_limit_bytes=56 << 20),
        name="front",
    )(clips, cot, gain, bias, weights)


def ring_peer(step):
    z, y, x, s, chan = coords()
    return s * ((z + step) % 4 * 8 + y * 2 + x) + (1 - s) * (z * 8 + (y + step) % 4 * 2 + x)


def cross_peer(step):
    z, y, x, s, chan = coords()
    return (1 - s) * ((z + step) % 4 * 8 + y * 2 + x) + s * (z * 8 + (y + step) % 4 * 2 + x)


def pair_peer():
    z, y, x, s, chan = coords()
    return z * 8 + y * 2 + 1 - x


def reduce_kernel(d_ref, small_ref, f_ref, small_out, slot_a, slot_b, from_left, from_right, stage_r, stage_l, mine, theirs,
                  small_1, small_2, small_3, sends, recvs, local_sem, s_sends, s_recvs):
    z, y, x, s, chan = coords()
    ring = s * z + (1 - s) * y
    cross = s * y + (1 - s) * z
    right, left, opp = ring_peer(1), ring_peer(3), ring_peer(2)
    up, down, far = cross_peer(1), cross_peer(3), cross_peer(2)
    pair = pair_peer()

    barrier = pltpu.get_barrier_semaphore()
    for peer in (right, left, opp, up, down, far, pair):
        pl.semaphore_signal(barrier, inc=1, device_id={"dp": peer}, device_id_type=MESH)
    pl.semaphore_wait(barrier, 7)

    started = []

    def send(src, dst, k, peer):
        copy = pltpu.make_async_remote_copy(src_ref=src, dst_ref=dst, send_sem=sends.at[k], recv_sem=recvs.at[k],
                                            device_id={"dp": peer}, device_id_type=MESH)
        copy.start()
        started.append(copy)
        return copy

    def blk(k):
        return (ring + k) % 4 * BLK

    H0, H1 = pl.ds(0, HALF), pl.ds(HALF, HALF)
    c0 = send(d_ref.at[pl.ds(blk(2), HALF)], slot_a, 0, right)
    c1 = send(d_ref.at[pl.ds(blk(2) + HALF, HALF)], slot_b, 1, left)
    c2 = send(d_ref.at[pl.ds(blk(1) + HALF, HALF)], from_left.at[H1], 2, right)
    c3 = send(d_ref.at[pl.ds(blk(3), HALF)], from_right.at[H0], 3, left)
    def small_stage(buf, peers, me, base, srcref):
        own = pltpu.make_async_copy(srcref, buf.at[me], local_sem.at[1])
        own.start()
        own.wait()
        cs = []
        for k, peer in enumerate(peers):
            c = pltpu.make_async_remote_copy(src_ref=srcref, dst_ref=buf.at[me], send_sem=s_sends.at[base + k],
                                             recv_sem=s_recvs.at[base + k], device_id={"dp": peer}, device_id_type=MESH)
            c.start()
            cs.append(c)
        return cs
    s1 = small_stage(small_1, (right, opp, left), ring, 0, small_ref)
    c0.wait_recv()
    stage_r[...] = (d_ref[pl.ds(blk(1), HALF)].astype(F32) + slot_a[...].astype(F32)).astype(BF)
    c4 = send(stage_r, from_left.at[H0], 4, right)
    c1.wait_recv()
    stage_l[...] = (d_ref[pl.ds(blk(3) + HALF, HALF)].astype(F32) + slot_b[...].astype(F32)).astype(BF)
    c5 = send(stage_l, from_right.at[H1], 5, left)
    c2.wait_recv()
    c3.wait_recv()
    c4.wait_recv()
    c5.wait_recv()
    mine[0] = (d_ref[pl.ds(blk(0), BLK)].astype(F32) + from_left[...].astype(F32)
               + from_right[...].astype(F32)).astype(BF)
    c6 = send(mine.at[0], theirs, 6, pair)
    c6.wait_recv()
    mine[1] = (mine[0].astype(F32) + theirs[...].astype(F32)).astype(BF)
    own = pltpu.make_async_copy(mine.at[1], f_ref.at[cross, pl.ds(blk(0), BLK)], local_sem.at[0])
    own.start()
    here = f_ref.at[cross, pl.ds(blk(0), BLK)]
    g_r = send(mine.at[1], here, 7, right)
    g_l = send(mine.at[1], here, 8, left)
    q_r = [send(mine.at[1], here, 9, up)]
    q_l = [send(mine.at[1], here, 10, down)]
    own.wait()

    def at(slab, k, h=None):
        if h is None:
            return f_ref.at[(cross + slab) % 4, pl.ds(blk(k), BLK)]
        return f_ref.at[(cross + slab) % 4, pl.ds(blk(k) + h * HALF, HALF)]
    g_r.wait_recv()
    f_r = send(at(0, 3, 0), at(0, 3, 0), 11, right)
    q_r.append(send(at(0, 3), at(0, 3), 12, up))
    q_l.append(send(at(0, 3), at(0, 3), 13, down))
    g_l.wait_recv()
    f_l = send(at(0, 1, 1), at(0, 1, 1), 14, left)
    q_r.append(send(at(0, 1), at(0, 1), 15, up))
    q_l.append(send(at(0, 1), at(0, 1), 16, down))
    q_r[0].wait_recv()
    hops = [send(at(3, 0, 0), at(3, 0, 0), 19, up)]
    q_l[0].wait_recv()
    hops.append(send(at(1, 0, 1), at(1, 0, 1), 20, down))
    f_r.wait_recv()
    f_l.wait_recv()
    q_r.append(send(at(0, 2), at(0, 2), 17, up))
    q_l.append(send(at(0, 2), at(0, 2), 18, down))
    for n, k in ((1, 3), (2, 1), (3, 2)):
        q_r[n].wait_recv()
        hops.append(send(at(3, k, 0), at(3, k, 0), 21 + 2 * (n - 1), up))
        q_l[n].wait_recv()
        hops.append(send(at(1, k, 1), at(1, k, 1), 22 + 2 * (n - 1), down))
    for c in s1:
        c.wait()
    small_2[4] = small_1[0] + small_1[1] + small_1[2] + small_1[3]
    s2 = small_stage(small_2, (up, far, down), cross, 3, small_2.at[4])
    for c in s2:
        c.wait()
    small_3[0] = small_2[0] + small_2[1] + small_2[2] + small_2[3]
    s3 = pltpu.make_async_remote_copy(src_ref=small_3.at[0], dst_ref=small_3.at[1], send_sem=s_sends.at[6],
                                      recv_sem=s_recvs.at[6], device_id={"dp": pair}, device_id_type=MESH)
    s3.start()
    s3.wait()
    small_out[...] = small_3[0] + small_3[1]
    for c in hops:
        c.wait_recv()
    for c in started:
        c.wait_send()


def reduce_gather(part, small):
    return pl.pallas_call(
        reduce_kernel,
        out_shape=(jax.ShapeDtypeStruct((4, UNITS, 16, SLICE), BF), jax.ShapeDtypeStruct((8, CH), F32)),
        in_specs=[pl.BlockSpec(memory_space=pltpu.VMEM)] * 2,
        out_specs=(pl.BlockSpec(memory_space=pl.ANY), pl.BlockSpec(memory_space=pltpu.VMEM)),
        scratch_shapes=[
            pltpu.VMEM((HALF, 16, SLICE), BF), pltpu.VMEM((HALF, 16, SLICE), BF),
            pltpu.VMEM((BLK, 16, SLICE), BF), pltpu.VMEM((BLK, 16, SLICE), BF),
            pltpu.VMEM((HALF, 16, SLICE), BF), pltpu.VMEM((HALF, 16, SLICE), BF),
            pltpu.VMEM((2, BLK, 16, SLICE), BF), pltpu.VMEM((BLK, 16, SLICE), BF),
            pltpu.VMEM((4, 8, CH), F32), pltpu.VMEM((5, 8, CH), F32), pltpu.VMEM((2, 8, CH), F32),
            pltpu.SemaphoreType.DMA((27,)), pltpu.SemaphoreType.DMA((27,)), pltpu.SemaphoreType.DMA((2,)),
            pltpu.SemaphoreType.DMA((7,)), pltpu.SemaphoreType.DMA((7,)),
        ],
        compiler_params=pltpu.CompilerParams(collective_id=2, has_side_effects=True, vmem_limit_bytes=56 << 20),
        name="reduce_gather",
    )(part, small)


def widen_kernel(slabs, out):
    rows = slabs.shape[1] * 16
    for k in range(4):
        out[:, k * SLICE : (k + 1) * SLICE] = slabs[k].reshape(rows, SLICE).astype(F32)


def widen(slabs):
    steps = 8
    units = UNITS // steps
    return pl.pallas_call(
        widen_kernel,
        grid=(steps,),
        out_shape=jax.ShapeDtypeStruct((UNITS * 16, FULL), F32),
        in_specs=[pl.BlockSpec((4, units, 16, SLICE), lambda i: (0, i, 0, 0))],
        out_specs=pl.BlockSpec((units * 16, FULL), lambda i: (i, 0)),
        name="widen",
    )(slabs)


def shards(clips, conv_weight, norm_gain, norm_bias, cotangent):
    part, small = front(
        clips.reshape(CH, POS), cotangent.reshape(CH, POS), norm_gain.reshape(CH, 1), norm_bias.reshape(CH, 1), conv_weight[0]
    )
    slabs, sums = reduce_gather(part, small)
    return widen(slabs).reshape(1, 27, CH, FULL), sums[0:1], sums[1:2]


def solution(mesh):
    in_specs = (
        P("dp", "chan", None, None),
        P("section", None, "chan", None),
        P("section", "chan"),
        P("section", "chan"),
        P("dp", "chan", None, None),
    )
    out_specs = (P("section", None, "chan", None), P("section", "chan"), P("section", "chan"))
    return jax.shard_map(shards, mesh=mesh, in_specs=in_specs, out_specs=out_specs, check_vma=False)
```

```python
import jax
import jax.numpy as jnp
from jax import lax
from jax.experimental import pallas as pl
from jax.experimental.pallas import tpu as pltpu
from jax.sharding import PartitionSpec as P

EPSILON = 1e-05
MESH = pl.DeviceIdType.MESH
BF = jnp.bfloat16
F32 = jnp.float32

CH = 256
FULL = 512
POS = 512
SLICE = 128
GROUP = 16
UNITS = 432
CHUNKS = 3
PART = UNITS // CHUNKS
BLK = PART // 4
HALF = BLK // 2


def coords():
    dp = lax.axis_index("dp")
    return dp // 8, dp // 2 % 4, dp % 2, lax.axis_index("section"), lax.axis_index("chan")


def remote(src, dst, send_sem, recv_sem, dp, section, chan):
    return pltpu.make_async_remote_copy(
        src_ref=src,
        dst_ref=dst,
        send_sem=send_sem,
        recv_sem=recv_sem,
        device_id={"dp": dp, "section": section, "chan": chan},
        device_id_type=MESH,
    )


def norm_frame(values):
    scale = 1.0 / (GROUP * 128)
    centre = jnp.sum(values, axis=(1, 2), keepdims=True) * scale
    moved = values - centre
    spread = jnp.sum(moved * moved, axis=(1, 2), keepdims=True) * scale
    inv_std = lax.rsqrt(spread + EPSILON)
    return moved * inv_std, inv_std


def norm_forward(act, gain, bias):
    grouped = act.reshape(GROUP, GROUP, POS)
    parts = [norm_frame(grouped[:, :, 128 * f : 128 * f + 128]) for f in range(4)]
    normed = jnp.concatenate([p[0] for p in parts], axis=2)
    shifted = jnp.concatenate([p[0] * gain + bias for p in parts], axis=2)
    return normed, shifted, [p[1] for p in parts]


def silu(shifted):
    return shifted * (1.0 / (1.0 + jnp.exp(-shifted)))


def norm_backward(grad_hidden, normed, shifted, inv_std, gain):
    sig = 1.0 / (1.0 + jnp.exp(-shifted))
    grad_shift = grad_hidden.reshape(GROUP, GROUP, POS) * sig * (1.0 + shifted * (1.0 - sig))
    gain_term = jnp.sum(grad_shift * normed, axis=2, keepdims=True)
    bias_term = jnp.sum(grad_shift, axis=2, keepdims=True)
    grad_normed = jnp.concatenate([grad_shift[:, :, 128 * f : 128 * f + 128] * gain for f in range(4)], axis=2)
    return grad_normed, gain_term, bias_term


def norm_input_grad(grad_normed, normed, inv_std):
    scale = 1.0 / (GROUP * 128)
    parts = []
    for f in range(4):
        g, n = grad_normed[:, :, 128 * f : 128 * f + 128], normed[:, :, 128 * f : 128 * f + 128]
        mean_grad = jnp.sum(g, axis=(1, 2), keepdims=True) * scale
        mean_cross = jnp.sum(g * n, axis=(1, 2), keepdims=True) * scale
        parts.append((g - mean_grad - n * mean_cross) * inv_std[f])
    return jnp.concatenate(parts, axis=2)


def small_rows(gain_term, bias_term):
    lane = lax.broadcasted_iota(jnp.int32, (CH, 128), 1)
    gain_col = jnp.broadcast_to(gain_term.reshape(CH, 1), (CH, 128))
    bias_col = jnp.broadcast_to(bias_term.reshape(CH, 1), (CH, 128))
    both = jnp.where(lane == 0, gain_col, jnp.where(lane == 1, bias_col, 0.0))
    return both.T[:8]


def shifted_columns(values, store):
    col = lax.broadcasted_iota(jnp.int32, values.shape, 0) % 16
    store(0, jnp.where(col == 0, 0.0, pltpu.roll(values, 1, 0)))
    store(1, values)
    store(2, jnp.where(col == 15, 0.0, pltpu.roll(values, POS - 1, 0)))


def column(row):
    return jnp.broadcast_to(row, (128, CH)).T.reshape(GROUP, GROUP, 128)


def conv_forward(lattice, weights, start, acc, wait_weights):
    for t in (2, 1, 0):
        wait_weights(t)
        rows = 128 * (t + 2)

        def tap_row(r, carry, t=t, rows=rows):
            lhs = lattice[0 : t + 2, pl.ds(r, 8), :, 0 : 3 * CH].reshape(rows, 3 * CH)
            rhs = weights[pl.ds(9 * t + 3 * r, 3), :, pl.ds(start, CH)].reshape(3 * CH, CH)
            part = jnp.dot(lhs, rhs, preferred_element_type=F32)
            acc[pl.ds(128 * (2 - t), rows)] = acc[pl.ds(128 * (2 - t), rows)] + part
            return carry

        lax.fori_loop(0, 3, tap_row, 0)


def conv_transposed(lattice, weights, acc, wait_weights, steps=(2, 1, 0)):
    for t in steps:
        wait_weights(t)
        cols = 128 * (t + 2)

        def tap_row(r, carry, t=t, cols=cols):
            part = None
            for v in range(3):
                rhs = lattice[2 - t : 4, pl.ds(2 - r, 8), :, v * FULL : (v + 1) * FULL].reshape(cols, FULL)
                one = lax.dot_general(
                    weights[9 * t + 3 * r + 2 - v], rhs, (((1,), (1,)), ((), ())), preferred_element_type=F32
                )
                part = one if part is None else part + one
            acc[:, 0:cols] = acc[:, 0:cols] + part
            return carry

        lax.fori_loop(0, 3, tap_row, 0)


def weight_gradient(hidden_all, lattice, out, steps):
    for t in steps:
        cols = 128 * (t + 2)
        lhs = jnp.concatenate([hidden_all[:, POS * k : POS * k + cols] for k in range(4)], axis=1)

        def tap_row(r, carry, t=t, cols=cols, lhs=lhs):
            rhs = lattice[:, 2 - t : 4, pl.ds(2 - r, 8)].reshape(4 * cols, 3 * SLICE)
            part = jnp.dot(lhs, rhs, preferred_element_type=F32).astype(BF)
            for v in range(3):
                tap = 9 * t + 3 * r + 2 - v
                out[pl.ds(16 * tap, 16)] = part[:, v * SLICE : (v + 1) * SLICE].reshape(16, 16, SLICE)
            return carry

        lax.fori_loop(0, 3, tap_row, 0)


def ring_add(*terms):
    total = terms[0].astype(F32)
    for term in terms[1:]:
        total = total + term.astype(F32)
    return total.astype(BF)


def step_kernel(
    clips_ref, cot_ref, gain_ref, bias_ref, w_hbm, f_ref, small_out,
    weights, lattice, slice_lattice, hidden_own, hidden_all, adj_own, full, slices, conv_out, conv_in, acc_y, acc_g, normed_s, inv_s,
    small_own, small_1, small_2, small_3, d_ref, slot_a, slot_b, from_left, from_right, stage_r, stage_l, mine, theirs,
    w_sems, own_sems, full_send, full_recv, slice_send, slice_recv, hid_send, hid_recv, y_send, y_recv,
    sends, recvs, keep_sems, s_sends, s_recvs,
):
    z, y, x, section, chan = coords()
    here = z * 8 + y * 2 + x

    def at_z(k):
        return k * 8 + y * 2 + x

    def at_y(k):
        return z * 8 + k * 2 + x

    barrier = pltpu.get_barrier_semaphore()

    def greet(dp, s, c):
        pl.semaphore_signal(barrier, inc=1, device_id={"dp": dp, "section": s, "chan": c}, device_id_type=MESH)

    for s in (0, 1):
        for c in (0, 1):
            for step in (1, 2, 3):
                greet(at_z((z + step) % 4), s, c)
                greet(at_y((y + step) % 4), s, c)
    greet(here, 1 - section, chan)
    greet(here, section, 1 - chan)
    greet(here, 1 - section, 1 - chan)
    greet(z * 8 + y * 2 + 1 - x, section, chan)

    def w_copy(t):
        return pltpu.make_async_copy(w_hbm.at[pl.ds(9 * t, 9)], weights.at[pl.ds(9 * t, 9)], w_sems.at[t])

    for t in (2, 1, 0):
        w_copy(t).start()

    def wait_weights(t):
        w_copy(t).wait()

    gain = column(gain_ref[...])
    bias = column(bias_ref[...])

    group = section * y + (1 - section) * z

    def ring(k):
        return section * at_y(k) + (1 - section) * at_z(k)

    def hidden_copy(step):
        return remote(
            hidden_own, hidden_all.at[:, pl.ds(pl.multiple_of(group * POS, POS), POS)],
            hid_send.at[step - 1], hid_recv.at[(4 - step) % 4], ring((group + step) % 4), section, chan,
        )

    def hidden_own_copy():
        return pltpu.make_async_copy(
            hidden_own, hidden_all.at[:, pl.ds(pl.multiple_of(group * POS, POS), POS)], own_sems.at[0]
        )

    def full_copy(c):
        return remote(adj_own, full.at[chan], full_send.at[c], full_recv.at[chan], here, 0, c)

    def cot_full_copy():
        return remote(adj_own, full.at[chan], full_send.at[0], full_recv.at[chan], here, 1, 1 - chan)

    def slice_copy(jj, c, dest_section):
        j = 2 * chan + jj
        slot = dest_section * y + (1 - dest_section) * z
        dp = dest_section * at_y(j) + (1 - dest_section) * at_z(j)
        return remote(
            adj_own.at[:, pl.ds(SLICE * jj, SLICE)], slices.at[slot], slice_send.at[2 * jj + c],
            slice_recv.at[slot], dp, dest_section, c,
        )

    def own_slice_copy():
        return pltpu.make_async_copy(
            adj_own.at[:, pl.ds(pl.multiple_of(y % 2 * SLICE, SLICE), SLICE)], slices.at[y], own_sems.at[1]
        )

    def conv_half(hh):
        return hh * chan + (1 - hh) * (1 - chan)

    def conv_copy(hh):
        return remote(conv_out.at[hh], conv_in.at[chan], y_send.at[hh], y_recv.at[chan], here, 1, conv_half(hh))

    zero_row = jnp.zeros((4, 1, 16, 3 * FULL), BF)
    lattice[:, 0:1] = zero_row
    lattice[:, 9:10] = zero_row
    zero_slice = jnp.zeros((4, 4, 1, 16, 3 * SLICE), BF)
    slice_lattice[:, :, 0:1] = zero_slice
    slice_lattice[:, :, 9:10] = zero_slice

    def fill_full(which, width, values):
        def store(v, moved):
            start = v * width + which
            lattice[:, 1:9, :, start : start + CH] = moved.astype(BF).reshape(4, 8, 16, CH)

        shifted_columns(values, store)

    @pl.when(section == 0)
    def _():
        normed, shifted, inv_std = norm_forward(clips_ref[...].astype(F32), gain, bias)
        hidden_own[...] = silu(shifted).astype(BF).reshape(CH, POS)
        normed_s[...] = normed
        for f in range(4):
            inv_s[f] = jnp.broadcast_to(inv_std[f], (GROUP, 1, 128))

    @pl.when(section == 1)
    def _():
        adj_own[...] = cot_ref[...].astype(F32).T.astype(BF)

    pl.semaphore_wait(barrier, 28)

    @pl.when(section == 0)
    def _():
        for step in (1, 2, 3):
            hidden_copy(step).start()
        hidden_own_copy().start()
        fill_full(0, CH, hidden_own[...].astype(F32).T)
        for hh in range(2):
            acc_y[...] = jnp.zeros_like(acc_y)
            start = pl.multiple_of(conv_half(hh) * CH, CH)
            conv_forward(lattice, weights, start, acc_y, wait_weights if hh == 0 else (lambda t: None))
            conv_out[hh] = acc_y[...].astype(BF)
            conv_copy(hh).start()

    @pl.when(section == 1)
    def _():
        cot_full_copy().start()
        for jj in range(2):
            for c in range(2):

                @pl.when((2 * chan + jj != y) | (chan != c))
                def _(jj=jj, c=c):
                    slice_copy(jj, c, 1).start()

        @pl.when(y // 2 == chan)
        def _():
            own_slice_copy().start()

        full[chan] = adj_own[...]
        remote(adj_own, full.at[1 - chan], full_send.at[0], full_recv.at[1 - chan], here, 1, 1 - chan).wait_recv()
        for c in range(2):
            fill_full(c * CH, FULL, full[c].astype(F32))
        acc_g[...] = jnp.zeros_like(acc_g)
        conv_transposed(lattice, weights, acc_g, wait_weights)
        for c in range(2):
            remote(conv_out.at[c], conv_in.at[c], y_send.at[c], y_recv.at[c], here, 1, c).wait_recv()
        summed = conv_in[0].astype(F32) + conv_in[1].astype(F32)
        act = (clips_ref[...].astype(F32) + summed.T).astype(BF).astype(F32)
        normed, shifted, inv_std = norm_forward(act, gain, bias)
        hidden_own[...] = silu(shifted).astype(BF).reshape(CH, POS)
        for step in (1, 2, 3):
            hidden_copy(step).start()
        hidden_own_copy().start()
        grad_normed, gain_term, bias_term = norm_backward(acc_g[...], normed, shifted, inv_std, gain)
        small_own[...] = small_rows(gain_term, bias_term)
        grad_act = norm_input_grad(grad_normed, normed, inv_std).reshape(CH, POS)
        adjoint = (cot_ref[...].astype(F32) + grad_act).T.astype(BF)
        cot_full_copy().wait_send()
        for jj in range(2):
            for c in range(2):

                @pl.when((2 * chan + jj != y) | (chan != c))
                def _(jj=jj, c=c):
                    slice_copy(jj, c, 1).wait_send()

        @pl.when(y // 2 == chan)
        def _():
            own_slice_copy().wait()

        adj_own[...] = adjoint
        for jj in range(2):
            for c in range(2):
                slice_copy(jj, c, 0).start()
        for c in range(2):
            full_copy(c).start()
        for k in range(4):

            @pl.when((k != y) | (y // 2 != chan))
            def _(k=k):
                remote(
                    adj_own.at[:, pl.ds(0, SLICE)], slices.at[k], slice_send.at[0], slice_recv.at[k], here, 1, 1 - chan
                ).wait_recv()

    @pl.when(section == 0)
    def _():
        for k in range(4):
            remote(
                adj_own.at[:, pl.ds(0, SLICE)], slices.at[k], slice_send.at[0], slice_recv.at[k], here, 1, chan
            ).wait_recv()

    for k in range(4):

        def store(v, moved, k=k):
            slice_lattice[k, :, 1:9, :, v * SLICE : (v + 1) * SLICE] = moved.astype(BF).reshape(4, 8, 16, SLICE)

        shifted_columns(slices[k].astype(F32), store)
    hidden_own_copy().wait()
    for step in (1, 2, 3):
        came = (group + step) % 4
        remote(
            hidden_own, hidden_all.at[:, pl.ds(pl.multiple_of(came * POS, POS), POS)],
            hid_send.at[step - 1], hid_recv.at[step], ring((group + step) % 4), section, chan,
        ).wait_recv()

    turn = section * z + (1 - section) * y

    def along(step):
        return section * at_z((z + step) % 4) + (1 - section) * at_y((y + step) % 4)

    def across(step):
        return section * at_y((y + step) % 4) + (1 - section) * at_z((z + step) % 4)

    right, left, opp = along(1), along(3), along(2)
    up, down, far = across(1), across(3), across(2)
    pair = z * 8 + y * 2 + 1 - x
    H0, H1 = pl.ds(0, HALF), pl.ds(HALF, HALF)
    started = []

    class Chunk:
        def __init__(self, n):
            self.n, self.base, self.copies = n, PART * (2 - n), {}

        def send(self, key, src, dst, dp):
            k = len(self.copies)
            copy = remote(src, dst, sends.at[self.n, k], recvs.at[self.n, k], dp, section, chan)
            copy.start()
            self.copies[key] = copy
            started.append(copy)

        def arrive(self, key):
            self.copies[key].wait_recv()

        def own(self, k, h=None):
            start = self.base + (turn + k) % 4 * BLK
            return pl.ds(start, BLK) if h is None else pl.ds(start + h * HALF, HALF)

        def slab(self, j, k, h=None):
            return f_ref.at[(group + j) % 4, self.own(k, h)]

        def reduce_start(self):
            n = self.n
            self.send("ra", d_ref.at[self.own(2, 0)], slot_a.at[n], right)
            self.send("rb", d_ref.at[self.own(2, 1)], slot_b.at[n], left)
            self.send("r1", d_ref.at[self.own(1, 1)], from_left.at[n, H1], right)
            self.send("l0", d_ref.at[self.own(3, 0)], from_right.at[n, H0], left)

        def reduce_hop(self):
            n = self.n
            self.arrive("ra")
            stage_r[n] = ring_add(d_ref[self.own(1, 0)], slot_a[n])
            self.send("r0", stage_r.at[n], from_left.at[n, H0], right)
            self.arrive("rb")
            stage_l[n] = ring_add(d_ref[self.own(3, 1)], slot_b[n])
            self.send("l1", stage_l.at[n], from_right.at[n, H1], left)

        def reduce_end(self):
            n = self.n
            for key in ("r1", "l0", "r0", "l1"):
                self.arrive(key)
            mine[n, 0] = ring_add(d_ref[self.own(0)], from_left[n], from_right[n])
            self.send("p", mine.at[n, 0], theirs.at[n], pair)

        def keep(self):
            return pltpu.make_async_copy(mine.at[self.n, 1], self.slab(0, 0), keep_sems.at[self.n])

        def gather_start(self):
            n = self.n
            self.arrive("p")
            mine[n, 1] = ring_add(mine[n, 0], theirs[n])
            block = mine.at[n, 1]
            self.send("gr", block, self.slab(0, 0), right)
            self.send("gl", block, self.slab(0, 0), left)
            self.send("u0", block, self.slab(0, 0), up)
            self.send("d0", block, self.slab(0, 0), down)
            self.keep().start()

        def spread(self, k):
            self.send(f"u{k}", self.slab(0, k), self.slab(0, k), up)
            self.send(f"d{k}", self.slab(0, k), self.slab(0, k), down)

        def gather_hop(self):
            self.arrive("gr")
            self.send("hr", self.slab(0, 3, 0), self.slab(0, 3, 0), right)
            self.arrive("gl")
            self.send("hl", self.slab(0, 1, 1), self.slab(0, 1, 1), left)
            self.spread(3)
            self.spread(1)
            self.pass_on(0)

        def pass_on(self, k):
            self.arrive(f"u{k}")
            self.send(f"uu{k}", self.slab(3, k, 0), self.slab(3, k, 0), up)
            self.arrive(f"d{k}")
            self.send(f"dd{k}", self.slab(1, k, 1), self.slab(1, k, 1), down)

        def gather_end(self):
            self.arrive("hr")
            self.arrive("hl")
            self.spread(2)
            self.pass_on(3)
            self.pass_on(1)

        def last(self):
            self.pass_on(2)
            for k in range(4):
                self.arrive(f"uu{k}")
                self.arrive(f"dd{k}")
            self.keep().wait()

    a, b, c = Chunk(0), Chunk(1), Chunk(2)
    weight_gradient(hidden_all, slice_lattice, d_ref, (2,))
    a.reduce_start()
    weight_gradient(hidden_all, slice_lattice, d_ref, (1,))
    b.reduce_start()
    a.reduce_hop()
    weight_gradient(hidden_all, slice_lattice, d_ref, (0,))
    c.reduce_start()
    b.reduce_hop()
    a.reduce_end()

    @pl.when(section == 0)
    def _():
        for k in range(2):
            remote(adj_own, full.at[k], full_send.at[k], full_recv.at[k], here, 1, chan).wait_recv()
            fill_full(k * CH, FULL, full[k].astype(F32))
        acc_g[...] = jnp.zeros_like(acc_g)

    c.reduce_hop()
    b.reduce_end()
    a.gather_start()

    @pl.when(section == 0)
    def _():
        conv_transposed(lattice, weights, acc_g, lambda t: None, (2,))

    c.reduce_end()
    b.gather_start()
    a.gather_hop()

    @pl.when(section == 0)
    def _():
        conv_transposed(lattice, weights, acc_g, lambda t: None, (1,))

    c.gather_start()
    b.gather_hop()
    a.gather_end()

    @pl.when(section == 0)
    def _():
        conv_transposed(lattice, weights, acc_g, lambda t: None, (0,))

    c.gather_hop()
    b.gather_end()

    @pl.when(section == 0)
    def _():
        normed = normed_s[...]
        shifted = jnp.concatenate([normed[:, :, 128 * f : 128 * f + 128] * gain + bias for f in range(4)], axis=2)
        inv_std = [inv_s[f] for f in range(4)]
        unused, gain_term, bias_term = norm_backward(acc_g[...], normed, shifted, inv_std, gain)
        small_own[...] = small_rows(gain_term, bias_term)

    def small_copies(buf, peers, slot, base, src):
        buf[slot] = src[...]
        copies = []
        for k, dp in enumerate(peers):
            copies.append(remote(src, buf.at[slot], s_sends.at[base + k], s_recvs.at[base + k], dp, section, chan))
        for copy in copies:
            copy.start()
        return copies

    first = small_copies(small_1, (right, opp, left), turn, 0, small_own)
    c.gather_end()
    a.last()
    for copy in first:
        copy.wait()
    small_2[4] = small_1[0] + small_1[1] + small_1[2] + small_1[3]
    second = small_copies(small_2, (up, far, down), group, 3, small_2.at[4])
    b.last()
    for copy in second:
        copy.wait()
    small_3[0] = small_2[0] + small_2[1] + small_2[2] + small_2[3]
    third = remote(small_3.at[0], small_3.at[1], s_sends.at[6], s_recvs.at[6], pair, section, chan)
    third.start()
    c.last()
    third.wait()
    small_out[...] = small_3[0] + small_3[1]

    @pl.when(section == 0)
    def _():
        for hh in range(2):
            conv_copy(hh).wait_send()

    @pl.when(section == 1)
    def _():
        for jj in range(2):
            for k in range(2):
                slice_copy(jj, k, 0).wait_send()
        for k in range(2):
            full_copy(k).wait_send()

    for step in (1, 2, 3):
        hidden_copy(step).wait_send()
    for copy in started:
        copy.wait_send()


def step(clips, cot, gain, bias, weights):
    vmem = pl.BlockSpec(memory_space=pltpu.VMEM)
    dma = pltpu.SemaphoreType.DMA
    return pl.pallas_call(
        step_kernel,
        out_shape=(jax.ShapeDtypeStruct((4, UNITS, 16, SLICE), BF), jax.ShapeDtypeStruct((8, CH), F32)),
        in_specs=[vmem, vmem, vmem, vmem, pl.BlockSpec(memory_space=pl.ANY)],
        out_specs=(pl.BlockSpec(memory_space=pl.ANY), vmem),
        scratch_shapes=[
            pltpu.VMEM((27, CH, FULL), BF),
            pltpu.VMEM((4, 10, 16, 3 * FULL), BF),
            pltpu.VMEM((4, 4, 10, 16, 3 * SLICE), BF),
            pltpu.VMEM((CH, POS), BF),
            pltpu.VMEM((CH, 4 * POS), BF),
            pltpu.VMEM((POS, CH), BF),
            pltpu.VMEM((2, POS, CH), BF),
            pltpu.VMEM((4, POS, SLICE), BF),
            pltpu.VMEM((2, POS, CH), BF),
            pltpu.VMEM((2, POS, CH), BF),
            pltpu.VMEM((POS, CH), F32),
            pltpu.VMEM((CH, POS), F32),
            pltpu.VMEM((GROUP, GROUP, POS), F32),
            pltpu.VMEM((4, GROUP, 1, 128), F32),
            pltpu.VMEM((8, CH), F32),
            pltpu.VMEM((4, 8, CH), F32),
            pltpu.VMEM((5, 8, CH), F32),
            pltpu.VMEM((2, 8, CH), F32),
            pltpu.VMEM((UNITS, 16, SLICE), BF),
            pltpu.VMEM((CHUNKS, HALF, 16, SLICE), BF),
            pltpu.VMEM((CHUNKS, HALF, 16, SLICE), BF),
            pltpu.VMEM((CHUNKS, BLK, 16, SLICE), BF),
            pltpu.VMEM((CHUNKS, BLK, 16, SLICE), BF),
            pltpu.VMEM((CHUNKS, HALF, 16, SLICE), BF),
            pltpu.VMEM((CHUNKS, HALF, 16, SLICE), BF),
            pltpu.VMEM((CHUNKS, 2, BLK, 16, SLICE), BF),
            pltpu.VMEM((CHUNKS, BLK, 16, SLICE), BF),
            dma((3,)), dma((2,)), dma((2,)), dma((2,)), dma((4,)), dma((4,)), dma((3,)), dma((4,)), dma((2,)), dma((2,)),
            dma((CHUNKS, 27)), dma((CHUNKS, 27)), dma((CHUNKS,)), dma((7,)), dma((7,)),
        ],
        compiler_params=pltpu.CompilerParams(collective_id=1, has_side_effects=True, vmem_limit_bytes=56 << 20),
        name="step",
    )(clips, cot, gain, bias, weights)


def widen_kernel(slabs, sums, out, gain_out, bias_out):
    rows = slabs.shape[1] * 16
    for k in range(4):
        out[:, k * SLICE : (k + 1) * SLICE] = slabs[k].reshape(rows, SLICE).astype(F32)
    gain_out[...] = sums[0:1]
    bias_out[...] = sums[1:2]


def widen(slabs, sums):
    steps = 16
    units = UNITS // steps
    row = pl.BlockSpec((1, CH), lambda i: (0, 0))
    return pl.pallas_call(
        widen_kernel,
        grid=(steps,),
        out_shape=(
            jax.ShapeDtypeStruct((UNITS * 16, FULL), F32),
            jax.ShapeDtypeStruct((1, CH), F32),
            jax.ShapeDtypeStruct((1, CH), F32),
        ),
        in_specs=[
            pl.BlockSpec((4, units, 16, SLICE), lambda i: (0, i, 0, 0)),
            pl.BlockSpec((8, CH), lambda i: (0, 0)),
        ],
        out_specs=(pl.BlockSpec((units * 16, FULL), lambda i: (i, 0)), row, row),
        name="widen",
    )(slabs, sums)


def shards(clips, conv_weight, norm_gain, norm_bias, cotangent):
    slabs, sums = step(clips.reshape(CH, POS), cotangent.reshape(CH, POS), norm_gain, norm_bias, conv_weight[0])
    weight_grad, gain_grad, bias_grad = widen(slabs, sums)
    return weight_grad.reshape(1, 27, CH, FULL), gain_grad, bias_grad


def solution(mesh):
    in_specs = (
        P("dp", "chan", None, None),
        P("section", None, "chan", None),
        P("section", "chan"),
        P("section", "chan"),
        P("dp", "chan", None, None),
    )
    out_specs = (P("section", None, "chan", None), P("section", "chan"), P("section", "chan"))
    return jax.shard_map(shards, mesh=mesh, in_specs=in_specs, out_specs=out_specs, check_vma=False)
```

```python
import jax
import jax.numpy as jnp
from jax import lax
from jax.experimental import pallas as pl
from jax.experimental.pallas import tpu as pltpu
from jax.sharding import PartitionSpec as P

EPSILON = 1e-05
MESH = pl.DeviceIdType.MESH
BF = jnp.bfloat16
F32 = jnp.float32

CH = 256
FULL = 512
POS = 512
SLICE = 128
GROUP = 16
UNITS = 432
CHUNKS = 3
PART = UNITS // CHUNKS
BLK = PART // 4
HALF = BLK // 2
WIDEN = 8


def coords():
    dp = lax.axis_index("dp")
    return dp // 8, dp // 2 % 4, dp % 2, lax.axis_index("section"), lax.axis_index("chan")


def remote(src, dst, send_sem, recv_sem, dp, section, chan):
    return pltpu.make_async_remote_copy(
        src_ref=src,
        dst_ref=dst,
        send_sem=send_sem,
        recv_sem=recv_sem,
        device_id={"dp": dp, "section": section, "chan": chan},
        device_id_type=MESH,
    )


def norm_frame(values):
    scale = 1.0 / (GROUP * 128)
    centre = jnp.sum(values, axis=(1, 2), keepdims=True) * scale
    moved = values - centre
    spread = jnp.sum(moved * moved, axis=(1, 2), keepdims=True) * scale
    inv_std = lax.rsqrt(spread + EPSILON)
    return moved * inv_std, inv_std


def norm_forward(act, gain, bias):
    grouped = act.reshape(GROUP, GROUP, POS)
    parts = [norm_frame(grouped[:, :, 128 * f : 128 * f + 128]) for f in range(4)]
    normed = jnp.concatenate([p[0] for p in parts], axis=2)
    shifted = jnp.concatenate([p[0] * gain + bias for p in parts], axis=2)
    return normed, shifted, [p[1] for p in parts]


def silu(shifted):
    return shifted * (1.0 / (1.0 + jnp.exp(-shifted)))


def norm_backward(grad_hidden, normed, shifted, inv_std, gain):
    sig = 1.0 / (1.0 + jnp.exp(-shifted))
    grad_shift = grad_hidden.reshape(GROUP, GROUP, POS) * sig * (1.0 + shifted * (1.0 - sig))
    gain_term = jnp.sum(grad_shift * normed, axis=2, keepdims=True)
    bias_term = jnp.sum(grad_shift, axis=2, keepdims=True)
    grad_normed = jnp.concatenate([grad_shift[:, :, 128 * f : 128 * f + 128] * gain for f in range(4)], axis=2)
    return grad_normed, gain_term, bias_term


def norm_input_grad(grad_normed, normed, inv_std):
    scale = 1.0 / (GROUP * 128)
    parts = []
    for f in range(4):
        g, n = grad_normed[:, :, 128 * f : 128 * f + 128], normed[:, :, 128 * f : 128 * f + 128]
        mean_grad = jnp.sum(g, axis=(1, 2), keepdims=True) * scale
        mean_cross = jnp.sum(g * n, axis=(1, 2), keepdims=True) * scale
        parts.append((g - mean_grad - n * mean_cross) * inv_std[f])
    return jnp.concatenate(parts, axis=2)


def small_rows(gain_term, bias_term):
    lane = lax.broadcasted_iota(jnp.int32, (CH, 128), 1)
    gain_col = jnp.broadcast_to(gain_term.reshape(CH, 1), (CH, 128))
    bias_col = jnp.broadcast_to(bias_term.reshape(CH, 1), (CH, 128))
    both = jnp.where(lane == 0, gain_col, jnp.where(lane == 1, bias_col, 0.0))
    return both.T[:8]


def shifted_columns(values, store):
    col = lax.broadcasted_iota(jnp.int32, values.shape, 0) % 16
    store(0, jnp.where(col == 0, 0.0, pltpu.roll(values, 1, 0)))
    store(1, values)
    store(2, jnp.where(col == 15, 0.0, pltpu.roll(values, POS - 1, 0)))


def column(row):
    return jnp.broadcast_to(row, (128, CH)).T.reshape(GROUP, GROUP, 128)


def conv_forward(lattice, weights, start, acc, wait_weights):
    for t in (2, 1, 0):
        wait_weights(t)
        rows = 128 * (t + 2)

        def tap_row(r, carry, t=t, rows=rows):
            lhs = lattice[0 : t + 2, pl.ds(r, 8), :, 0 : 3 * CH].reshape(rows, 3 * CH)
            rhs = weights[pl.ds(9 * t + 3 * r, 3), :, pl.ds(start, CH)].reshape(3 * CH, CH)
            part = jnp.dot(lhs, rhs, preferred_element_type=F32)
            acc[pl.ds(128 * (2 - t), rows)] = acc[pl.ds(128 * (2 - t), rows)] + part
            return carry

        lax.fori_loop(0, 3, tap_row, 0)


def conv_transposed(lattice, weights, acc, wait_weights, steps=(2, 1, 0)):
    for t in steps:
        wait_weights(t)
        cols = 128 * (t + 2)

        def tap_row(r, carry, t=t, cols=cols):
            part = None
            for v in range(3):
                rhs = lattice[2 - t : 4, pl.ds(2 - r, 8), :, v * FULL : (v + 1) * FULL].reshape(cols, FULL)
                one = lax.dot_general(
                    weights[9 * t + 3 * r + 2 - v], rhs, (((1,), (1,)), ((), ())), preferred_element_type=F32
                )
                part = one if part is None else part + one
            acc[:, 0:cols] = acc[:, 0:cols] + part
            return carry

        lax.fori_loop(0, 3, tap_row, 0)


def weight_gradient(hidden_all, lattice, out, steps):
    for t in steps:
        cols = 128 * (t + 2)
        lhs = jnp.concatenate([hidden_all[:, POS * k : POS * k + cols] for k in range(4)], axis=1)

        def tap_row(r, carry, t=t, cols=cols, lhs=lhs):
            rhs = lattice[:, 2 - t : 4, pl.ds(2 - r, 8)].reshape(4 * cols, 3 * SLICE)
            part = jnp.dot(lhs, rhs, preferred_element_type=F32).astype(BF)
            for v in range(3):
                tap = 9 * t + 3 * r + 2 - v
                out[pl.ds(16 * tap, 16)] = part[:, v * SLICE : (v + 1) * SLICE].reshape(16, 16, SLICE)
            return carry

        lax.fori_loop(0, 3, tap_row, 0)


def ring_add(*terms):
    total = terms[0].astype(F32)
    for term in terms[1:]:
        total = total + term.astype(F32)
    return total.astype(BF)


def step_kernel(
    clips_ref, cot_ref, gain_ref, bias_ref, w_hbm, f_ref, small_out,
    weights, lattice, slice_lattice, hidden_own, hidden_all, adj_own, full, slices, conv_out, conv_in, acc_y, acc_g, normed_s, inv_s,
    small_own, small_1, small_2, small_3, d_ref, slot_a, slot_b, from_left, from_right, stage_r, stage_l, mine, theirs,
    w_sems, own_sems, full_send, full_recv, slice_send, slice_recv, hid_send, hid_recv, y_send, y_recv,
    sends, recvs, keep_sems, s_sends, s_recvs,
):
    z, y, x, section, chan = coords()
    here = z * 8 + y * 2 + x

    def at_z(k):
        return k * 8 + y * 2 + x

    def at_y(k):
        return z * 8 + k * 2 + x

    barrier = pltpu.get_barrier_semaphore()

    def greet(dp, s, c):
        pl.semaphore_signal(barrier, inc=1, device_id={"dp": dp, "section": s, "chan": c}, device_id_type=MESH)

    for s in (0, 1):
        for c in (0, 1):
            for step in (1, 2, 3):
                greet(at_z((z + step) % 4), s, c)
                greet(at_y((y + step) % 4), s, c)
    greet(here, 1 - section, chan)
    greet(here, section, 1 - chan)
    greet(here, 1 - section, 1 - chan)
    greet(z * 8 + y * 2 + 1 - x, section, chan)

    def w_copy(t):
        return pltpu.make_async_copy(w_hbm.at[pl.ds(9 * t, 9)], weights.at[pl.ds(9 * t, 9)], w_sems.at[t])

    for t in (2, 1, 0):
        w_copy(t).start()

    def wait_weights(t):
        w_copy(t).wait()

    gain = column(gain_ref[...])
    bias = column(bias_ref[...])

    group = section * y + (1 - section) * z

    def ring(k):
        return section * at_y(k) + (1 - section) * at_z(k)

    def hidden_copy(step):
        return remote(
            hidden_own, hidden_all.at[:, pl.ds(pl.multiple_of(group * POS, POS), POS)],
            hid_send.at[step - 1], hid_recv.at[(4 - step) % 4], ring((group + step) % 4), section, chan,
        )

    def hidden_own_copy():
        return pltpu.make_async_copy(
            hidden_own, hidden_all.at[:, pl.ds(pl.multiple_of(group * POS, POS), POS)], own_sems.at[0]
        )

    def full_copy(c):
        return remote(adj_own, full.at[chan], full_send.at[c], full_recv.at[chan], here, 0, c)

    def cot_full_copy():
        return remote(adj_own, full.at[chan], full_send.at[0], full_recv.at[chan], here, 1, 1 - chan)

    def slice_copy(jj, c, dest_section):
        j = 2 * chan + jj
        slot = dest_section * y + (1 - dest_section) * z
        dp = dest_section * at_y(j) + (1 - dest_section) * at_z(j)
        return remote(
            adj_own.at[:, pl.ds(SLICE * jj, SLICE)], slices.at[slot], slice_send.at[2 * jj + c],
            slice_recv.at[slot], dp, dest_section, c,
        )

    def own_slice_copy():
        return pltpu.make_async_copy(
            adj_own.at[:, pl.ds(pl.multiple_of(y % 2 * SLICE, SLICE), SLICE)], slices.at[y], own_sems.at[1]
        )

    def conv_half(hh):
        return hh * chan + (1 - hh) * (1 - chan)

    def conv_copy(hh):
        return remote(conv_out.at[hh], conv_in.at[chan], y_send.at[hh], y_recv.at[chan], here, 1, conv_half(hh))

    zero_row = jnp.zeros((4, 1, 16, 3 * FULL), BF)
    lattice[:, 0:1] = zero_row
    lattice[:, 9:10] = zero_row
    zero_slice = jnp.zeros((4, 4, 1, 16, 3 * SLICE), BF)
    slice_lattice[:, :, 0:1] = zero_slice
    slice_lattice[:, :, 9:10] = zero_slice

    def fill_full(which, width, values):
        def store(v, moved):
            start = v * width + which
            lattice[:, 1:9, :, start : start + CH] = moved.astype(BF).reshape(4, 8, 16, CH)

        shifted_columns(values, store)

    @pl.when(section == 0)
    def _():
        normed, shifted, inv_std = norm_forward(clips_ref[...].astype(F32), gain, bias)
        hidden_own[...] = silu(shifted).astype(BF).reshape(CH, POS)
        normed_s[...] = normed
        for f in range(4):
            inv_s[f] = jnp.broadcast_to(inv_std[f], (GROUP, 1, 128))

    @pl.when(section == 1)
    def _():
        adj_own[...] = cot_ref[...].astype(F32).T.astype(BF)

    pl.semaphore_wait(barrier, 28)

    @pl.when(section == 0)
    def _():
        for step in (1, 2, 3):
            hidden_copy(step).start()
        hidden_own_copy().start()
        fill_full(0, CH, hidden_own[...].astype(F32).T)
        for hh in range(2):
            acc_y[...] = jnp.zeros_like(acc_y)
            start = pl.multiple_of(conv_half(hh) * CH, CH)
            conv_forward(lattice, weights, start, acc_y, wait_weights if hh == 0 else (lambda t: None))
            conv_out[hh] = acc_y[...].astype(BF)
            conv_copy(hh).start()

    @pl.when(section == 1)
    def _():
        cot_full_copy().start()
        for jj in range(2):
            for c in range(2):

                @pl.when((2 * chan + jj != y) | (chan != c))
                def _(jj=jj, c=c):
                    slice_copy(jj, c, 1).start()

        @pl.when(y // 2 == chan)
        def _():
            own_slice_copy().start()

        full[chan] = adj_own[...]
        remote(adj_own, full.at[1 - chan], full_send.at[0], full_recv.at[1 - chan], here, 1, 1 - chan).wait_recv()
        for c in range(2):
            fill_full(c * CH, FULL, full[c].astype(F32))
        acc_g[...] = jnp.zeros_like(acc_g)
        conv_transposed(lattice, weights, acc_g, wait_weights)
        for c in range(2):
            remote(conv_out.at[c], conv_in.at[c], y_send.at[c], y_recv.at[c], here, 1, c).wait_recv()
        summed = conv_in[0].astype(F32) + conv_in[1].astype(F32)
        act = (clips_ref[...].astype(F32) + summed.T).astype(BF).astype(F32)
        normed, shifted, inv_std = norm_forward(act, gain, bias)
        hidden_own[...] = silu(shifted).astype(BF).reshape(CH, POS)
        for step in (1, 2, 3):
            hidden_copy(step).start()
        hidden_own_copy().start()
        grad_normed, gain_term, bias_term = norm_backward(acc_g[...], normed, shifted, inv_std, gain)
        small_own[...] = small_rows(gain_term, bias_term)
        grad_act = norm_input_grad(grad_normed, normed, inv_std).reshape(CH, POS)
        adjoint = (cot_ref[...].astype(F32) + grad_act).T.astype(BF)
        cot_full_copy().wait_send()
        for jj in range(2):
            for c in range(2):

                @pl.when((2 * chan + jj != y) | (chan != c))
                def _(jj=jj, c=c):
                    slice_copy(jj, c, 1).wait_send()

        @pl.when(y // 2 == chan)
        def _():
            own_slice_copy().wait()

        adj_own[...] = adjoint
        for jj in range(2):
            for c in range(2):
                slice_copy(jj, c, 0).start()
        for c in range(2):
            full_copy(c).start()
        for k in range(4):

            @pl.when((k != y) | (y // 2 != chan))
            def _(k=k):
                remote(
                    adj_own.at[:, pl.ds(0, SLICE)], slices.at[k], slice_send.at[0], slice_recv.at[k], here, 1, 1 - chan
                ).wait_recv()

    @pl.when(section == 0)
    def _():
        for k in range(4):
            remote(
                adj_own.at[:, pl.ds(0, SLICE)], slices.at[k], slice_send.at[0], slice_recv.at[k], here, 1, chan
            ).wait_recv()

    for k in range(4):

        def store(v, moved, k=k):
            slice_lattice[k, :, 1:9, :, v * SLICE : (v + 1) * SLICE] = moved.astype(BF).reshape(4, 8, 16, SLICE)

        shifted_columns(slices[k].astype(F32), store)
    hidden_own_copy().wait()
    for step in (1, 2, 3):
        came = (group + step) % 4
        remote(
            hidden_own, hidden_all.at[:, pl.ds(pl.multiple_of(came * POS, POS), POS)],
            hid_send.at[step - 1], hid_recv.at[step], ring((group + step) % 4), section, chan,
        ).wait_recv()

    turn = section * z + (1 - section) * y

    def along(step):
        return section * at_z((z + step) % 4) + (1 - section) * at_y((y + step) % 4)

    def across(step):
        return section * at_y((y + step) % 4) + (1 - section) * at_z((z + step) % 4)

    right, left, opp = along(1), along(3), along(2)
    up, down, far = across(1), across(3), across(2)
    pair = z * 8 + y * 2 + 1 - x
    H0, H1 = pl.ds(0, HALF), pl.ds(HALF, HALF)
    started = []

    class Chunk:
        def __init__(self, n):
            self.n, self.base, self.copies = n, PART * (2 - n), {}

        def send(self, key, src, dst, dp):
            k = len(self.copies)
            copy = remote(src, dst, sends.at[self.n, k], recvs.at[self.n, k], dp, section, chan)
            copy.start()
            self.copies[key] = copy
            started.append(copy)

        def arrive(self, key):
            self.copies[key].wait_recv()

        def own(self, k, h=None):
            start = self.base + (turn + k) % 4 * BLK
            return pl.ds(start, BLK) if h is None else pl.ds(start + h * HALF, HALF)

        def slab(self, j, k, h=None):
            return f_ref.at[(group + j) % 4, self.own(k, h)]

        def reduce_start(self):
            n = self.n
            self.send("ra", d_ref.at[self.own(2, 0)], slot_a.at[n], right)
            self.send("rb", d_ref.at[self.own(2, 1)], slot_b.at[n], left)
            self.send("r1", d_ref.at[self.own(1, 1)], from_left.at[n, H1], right)
            self.send("l0", d_ref.at[self.own(3, 0)], from_right.at[n, H0], left)

        def reduce_hop(self):
            n = self.n
            self.arrive("ra")
            stage_r[n] = ring_add(d_ref[self.own(1, 0)], slot_a[n])
            self.send("r0", stage_r.at[n], from_left.at[n, H0], right)
            self.arrive("rb")
            stage_l[n] = ring_add(d_ref[self.own(3, 1)], slot_b[n])
            self.send("l1", stage_l.at[n], from_right.at[n, H1], left)

        def reduce_end(self):
            n = self.n
            for key in ("r1", "l0", "r0", "l1"):
                self.arrive(key)
            mine[n, 0] = ring_add(d_ref[self.own(0)], from_left[n], from_right[n])
            self.send("p", mine.at[n, 0], theirs.at[n], pair)

        def keep(self):
            return pltpu.make_async_copy(mine.at[self.n, 1], self.slab(0, 0), keep_sems.at[self.n])

        def gather_start(self):
            n = self.n
            self.arrive("p")
            mine[n, 1] = ring_add(mine[n, 0], theirs[n])
            block = mine.at[n, 1]
            self.send("gr", block, self.slab(0, 0), right)
            self.send("gl", block, self.slab(0, 0), left)
            self.send("u0", block, self.slab(0, 0), up)
            self.send("d0", block, self.slab(0, 0), down)
            self.keep().start()

        def spread(self, k):
            self.send(f"u{k}", self.slab(0, k), self.slab(0, k), up)
            self.send(f"d{k}", self.slab(0, k), self.slab(0, k), down)

        def gather_hop(self):
            self.arrive("gr")
            self.send("hr", self.slab(0, 3, 0), self.slab(0, 3, 0), right)
            self.arrive("gl")
            self.send("hl", self.slab(0, 1, 1), self.slab(0, 1, 1), left)
            self.spread(3)
            self.spread(1)
            self.pass_on(0)

        def pass_on(self, k):
            self.arrive(f"u{k}")
            self.send(f"uu{k}", self.slab(3, k, 0), self.slab(3, k, 0), up)
            self.arrive(f"d{k}")
            self.send(f"dd{k}", self.slab(1, k, 1), self.slab(1, k, 1), down)

        def gather_end(self):
            self.arrive("hr")
            self.arrive("hl")
            self.spread(2)
            self.pass_on(3)
            self.pass_on(1)

        def last(self):
            self.pass_on(2)
            for k in range(4):
                self.arrive(f"uu{k}")
                self.arrive(f"dd{k}")
            self.keep().wait()

    a, b, c = Chunk(0), Chunk(1), Chunk(2)
    weight_gradient(hidden_all, slice_lattice, d_ref, (2,))
    a.reduce_start()
    weight_gradient(hidden_all, slice_lattice, d_ref, (1,))
    b.reduce_start()
    a.reduce_hop()
    weight_gradient(hidden_all, slice_lattice, d_ref, (0,))
    c.reduce_start()
    b.reduce_hop()
    a.reduce_end()

    @pl.when(section == 0)
    def _():
        for k in range(2):
            remote(adj_own, full.at[k], full_send.at[k], full_recv.at[k], here, 1, chan).wait_recv()
            fill_full(k * CH, FULL, full[k].astype(F32))
        acc_g[...] = jnp.zeros_like(acc_g)

    c.reduce_hop()
    b.reduce_end()
    a.gather_start()

    @pl.when(section == 0)
    def _():
        conv_transposed(lattice, weights, acc_g, lambda t: None, (2,))

    c.reduce_end()
    b.gather_start()
    a.gather_hop()

    @pl.when(section == 0)
    def _():
        conv_transposed(lattice, weights, acc_g, lambda t: None, (1,))

    c.gather_start()
    b.gather_hop()
    a.gather_end()

    @pl.when(section == 0)
    def _():
        conv_transposed(lattice, weights, acc_g, lambda t: None, (0,))

    c.gather_hop()
    b.gather_end()

    @pl.when(section == 0)
    def _():
        normed = normed_s[...]
        shifted = jnp.concatenate([normed[:, :, 128 * f : 128 * f + 128] * gain + bias for f in range(4)], axis=2)
        inv_std = [inv_s[f] for f in range(4)]
        unused, gain_term, bias_term = norm_backward(acc_g[...], normed, shifted, inv_std, gain)
        small_own[...] = small_rows(gain_term, bias_term)

    def small_copies(buf, peers, slot, base, src):
        buf[slot] = src[...]
        copies = []
        for k, dp in enumerate(peers):
            copies.append(remote(src, buf.at[slot], s_sends.at[base + k], s_recvs.at[base + k], dp, section, chan))
        for copy in copies:
            copy.start()
        return copies

    first = small_copies(small_1, (right, opp, left), turn, 0, small_own)
    c.gather_end()
    a.last()
    for copy in first:
        copy.wait()
    small_2[4] = small_1[0] + small_1[1] + small_1[2] + small_1[3]
    second = small_copies(small_2, (up, far, down), group, 3, small_2.at[4])
    b.last()
    for copy in second:
        copy.wait()
    small_3[0] = small_2[0] + small_2[1] + small_2[2] + small_2[3]
    third = remote(small_3.at[0], small_3.at[1], s_sends.at[6], s_recvs.at[6], pair, section, chan)
    third.start()
    c.last()
    third.wait()
    small_out[...] = small_3[0] + small_3[1]

    @pl.when(section == 0)
    def _():
        for hh in range(2):
            conv_copy(hh).wait_send()

    @pl.when(section == 1)
    def _():
        for jj in range(2):
            for k in range(2):
                slice_copy(jj, k, 0).wait_send()
        for k in range(2):
            full_copy(k).wait_send()

    for step in (1, 2, 3):
        hidden_copy(step).wait_send()
    for copy in started:
        copy.wait_send()


def step(clips, cot, gain, bias, weights):
    vmem = pl.BlockSpec(memory_space=pltpu.VMEM)
    dma = pltpu.SemaphoreType.DMA
    return pl.pallas_call(
        step_kernel,
        out_shape=(pltpu.VMEM((4, UNITS, 16, SLICE), BF), jax.ShapeDtypeStruct((8, CH), F32)),
        in_specs=[vmem, vmem, vmem, vmem, pl.BlockSpec(memory_space=pl.ANY)],
        out_specs=(vmem, vmem),
        scratch_shapes=[
            pltpu.VMEM((27, CH, FULL), BF),
            pltpu.VMEM((4, 10, 16, 3 * FULL), BF),
            pltpu.VMEM((4, 4, 10, 16, 3 * SLICE), BF),
            pltpu.VMEM((CH, POS), BF),
            pltpu.VMEM((CH, 4 * POS), BF),
            pltpu.VMEM((POS, CH), BF),
            pltpu.VMEM((2, POS, CH), BF),
            pltpu.VMEM((4, POS, SLICE), BF),
            pltpu.VMEM((2, POS, CH), BF),
            pltpu.VMEM((2, POS, CH), BF),
            pltpu.VMEM((POS, CH), F32),
            pltpu.VMEM((CH, POS), F32),
            pltpu.VMEM((GROUP, GROUP, POS), F32),
            pltpu.VMEM((4, GROUP, 1, 128), F32),
            pltpu.VMEM((8, CH), F32),
            pltpu.VMEM((4, 8, CH), F32),
            pltpu.VMEM((5, 8, CH), F32),
            pltpu.VMEM((2, 8, CH), F32),
            pltpu.VMEM((UNITS, 16, SLICE), BF),
            pltpu.VMEM((CHUNKS, HALF, 16, SLICE), BF),
            pltpu.VMEM((CHUNKS, HALF, 16, SLICE), BF),
            pltpu.VMEM((CHUNKS, BLK, 16, SLICE), BF),
            pltpu.VMEM((CHUNKS, BLK, 16, SLICE), BF),
            pltpu.VMEM((CHUNKS, HALF, 16, SLICE), BF),
            pltpu.VMEM((CHUNKS, HALF, 16, SLICE), BF),
            pltpu.VMEM((CHUNKS, 2, BLK, 16, SLICE), BF),
            pltpu.VMEM((CHUNKS, BLK, 16, SLICE), BF),
            dma((3,)), dma((2,)), dma((2,)), dma((2,)), dma((4,)), dma((4,)), dma((3,)), dma((4,)), dma((2,)), dma((2,)),
            dma((CHUNKS, 27)), dma((CHUNKS, 27)), dma((CHUNKS,)), dma((7,)), dma((7,)),
        ],
        compiler_params=pltpu.CompilerParams(collective_id=1, has_side_effects=True, vmem_limit_bytes=48 << 20),
        name="step",
    )(clips, cot, gain, bias, weights)


def widen_kernel(slabs, sums, out, gain_out, bias_out, rows_a, rows_b, sems):
    steps, units = WIDEN, UNITS // WIDEN
    rows = units * 16
    gain_out[...] = sums[0:1]
    bias_out[...] = sums[1:2]
    buffers = (rows_a, rows_b)

    def copy(i):
        return pltpu.make_async_copy(buffers[i % 2], out.at[pl.ds(i * rows, rows)], sems.at[i % 2])

    for i in range(steps):
        if i >= 2:
            copy(i - 2).wait()
        for k in range(4):
            buffers[i % 2][:, k * SLICE : (k + 1) * SLICE] = slabs[k, i * units : (i + 1) * units].reshape(rows, SLICE).astype(F32)
        copy(i).start()
    copy(steps - 2).wait()
    copy(steps - 1).wait()


def widen(slabs, sums):
    vmem = pl.BlockSpec(memory_space=pltpu.VMEM)
    rows = UNITS // WIDEN * 16
    return pl.pallas_call(
        widen_kernel,
        out_shape=(
            jax.ShapeDtypeStruct((UNITS * 16, FULL), F32),
            jax.ShapeDtypeStruct((1, CH), F32),
            jax.ShapeDtypeStruct((1, CH), F32),
        ),
        in_specs=[vmem, vmem],
        out_specs=(pl.BlockSpec(memory_space=pl.ANY), vmem, vmem),
        scratch_shapes=[pltpu.VMEM((rows, FULL), F32), pltpu.VMEM((rows, FULL), F32), pltpu.SemaphoreType.DMA((2,))],
        compiler_params=pltpu.CompilerParams(vmem_limit_bytes=20 << 20),
        name="widen",
    )(slabs, sums)


def shards(clips, conv_weight, norm_gain, norm_bias, cotangent):
    slabs, sums = step(clips.reshape(CH, POS), cotangent.reshape(CH, POS), norm_gain, norm_bias, conv_weight[0])
    weight_grad, gain_grad, bias_grad = widen(slabs, sums)
    return weight_grad.reshape(1, 27, CH, FULL), gain_grad, bias_grad


def solution(mesh):
    in_specs = (
        P("dp", "chan", None, None),
        P("section", None, "chan", None),
        P("section", "chan"),
        P("section", "chan"),
        P("dp", "chan", None, None),
    )
    out_specs = (P("section", None, "chan", None), P("section", "chan"), P("section", "chan"))
    return jax.shard_map(shards, mesh=mesh, in_specs=in_specs, out_specs=out_specs, check_vma=False)
```

```python
import jax
import jax.numpy as jnp
from jax import lax
from jax.experimental import pallas as pl
from jax.experimental.pallas import tpu as pltpu
from jax.sharding import PartitionSpec as P

EPSILON = 1e-05
MESH = pl.DeviceIdType.MESH
BF = jnp.bfloat16
F32 = jnp.float32

CH = 256
FULL = 512
POS = 512
SLICE = 128
GROUP = 16
UNITS = 432
CHUNKS = ((48, True), (48, False), (96, True), (96, False), (144, False))
WIDEN = 8


def coords():
    dp = lax.axis_index("dp")
    return dp // 8, dp // 2 % 4, dp % 2, lax.axis_index("section"), lax.axis_index("chan")


def remote(src, dst, send_sem, recv_sem, dp, section, chan):
    return pltpu.make_async_remote_copy(
        src_ref=src,
        dst_ref=dst,
        send_sem=send_sem,
        recv_sem=recv_sem,
        device_id={"dp": dp, "section": section, "chan": chan},
        device_id_type=MESH,
    )


def norm_frame(values):
    scale = 1.0 / (GROUP * 128)
    centre = jnp.sum(values, axis=(1, 2), keepdims=True) * scale
    moved = values - centre
    spread = jnp.sum(moved * moved, axis=(1, 2), keepdims=True) * scale
    inv_std = lax.rsqrt(spread + EPSILON)
    return moved * inv_std, inv_std


def norm_forward(act, gain, bias):
    grouped = act.reshape(GROUP, GROUP, POS)
    parts = [norm_frame(grouped[:, :, 128 * f : 128 * f + 128]) for f in range(4)]
    normed = jnp.concatenate([p[0] for p in parts], axis=2)
    shifted = jnp.concatenate([p[0] * gain + bias for p in parts], axis=2)
    return normed, shifted, [p[1] for p in parts]


def silu(shifted):
    return shifted * (1.0 / (1.0 + jnp.exp(-shifted)))


def norm_backward(grad_hidden, normed, shifted, inv_std, gain):
    sig = 1.0 / (1.0 + jnp.exp(-shifted))
    grad_shift = grad_hidden.reshape(GROUP, GROUP, POS) * sig * (1.0 + shifted * (1.0 - sig))
    gain_term = jnp.sum(grad_shift * normed, axis=2, keepdims=True)
    bias_term = jnp.sum(grad_shift, axis=2, keepdims=True)
    grad_normed = jnp.concatenate([grad_shift[:, :, 128 * f : 128 * f + 128] * gain for f in range(4)], axis=2)
    return grad_normed, gain_term, bias_term


def norm_input_grad(grad_normed, normed, inv_std):
    scale = 1.0 / (GROUP * 128)
    parts = []
    for f in range(4):
        g, n = grad_normed[:, :, 128 * f : 128 * f + 128], normed[:, :, 128 * f : 128 * f + 128]
        mean_grad = jnp.sum(g, axis=(1, 2), keepdims=True) * scale
        mean_cross = jnp.sum(g * n, axis=(1, 2), keepdims=True) * scale
        parts.append((g - mean_grad - n * mean_cross) * inv_std[f])
    return jnp.concatenate(parts, axis=2)


def small_rows(gain_term, bias_term):
    lane = lax.broadcasted_iota(jnp.int32, (CH, 128), 1)
    gain_col = jnp.broadcast_to(gain_term.reshape(CH, 1), (CH, 128))
    bias_col = jnp.broadcast_to(bias_term.reshape(CH, 1), (CH, 128))
    both = jnp.where(lane == 0, gain_col, jnp.where(lane == 1, bias_col, 0.0))
    return both.T[:8]


def shifted_columns(values, store):
    col = lax.broadcasted_iota(jnp.int32, values.shape, 0) % 16
    store(0, jnp.where(col == 0, 0.0, pltpu.roll(values, 1, 0)))
    store(1, values)
    store(2, jnp.where(col == 15, 0.0, pltpu.roll(values, POS - 1, 0)))


def column(row):
    return jnp.broadcast_to(row, (128, CH)).T.reshape(GROUP, GROUP, 128)


def conv_forward(lattice, weights, start, acc, wait_weights):
    for t in (2, 1, 0):
        wait_weights(t)
        rows = 128 * (t + 2)

        def tap_row(r, carry, t=t, rows=rows):
            lhs = lattice[0, 0 : t + 2, pl.ds(r, 8)].reshape(rows, 3 * CH)
            rhs = weights[pl.ds(9 * t + 3 * r, 3), :, pl.ds(start, CH)].reshape(3 * CH, CH)
            part = jnp.dot(lhs, rhs, preferred_element_type=F32)
            acc[pl.ds(128 * (2 - t), rows)] = acc[pl.ds(128 * (2 - t), rows)] + part
            return carry

        lax.fori_loop(0, 3, tap_row, 0)


def conv_transposed(lattice, weights, half, acc, wait_weights, steps=(2, 1, 0)):
    start = pl.multiple_of(half * CH, CH)
    for t in steps:
        wait_weights(t)
        cols = 128 * (t + 2)

        def tap_row(r, carry, t=t, cols=cols):
            part = None
            for v in range(3):
                rhs = lattice[half, 2 - t : 4, pl.ds(2 - r, 8), :, v * CH : (v + 1) * CH].reshape(cols, CH)
                one = lax.dot_general(
                    weights[9 * t + 3 * r + 2 - v, :, pl.ds(start, CH)], rhs, (((1,), (1,)), ((), ())),
                    preferred_element_type=F32,
                )
                part = one if part is None else part + one
            acc[:, 0:cols] = acc[:, 0:cols] + part
            return carry

        lax.fori_loop(0, 3, tap_row, 0)


def weight_gradient(hidden_all, lattice, out, t, first, count):
    cols = 128 * (t + 2)
    lhs = jnp.concatenate([hidden_all[:, POS * k : POS * k + cols] for k in range(4)], axis=1)

    def tap_row(step, carry):
        r = first - step
        rhs = lattice[:, 2 - t : 4, pl.ds(2 - r, 8)].reshape(4 * cols, 3 * SLICE)
        part = jnp.dot(lhs, rhs, preferred_element_type=F32).astype(BF)
        for v in range(3):
            tap = 9 * t + 3 * r + 2 - v
            out[pl.ds(16 * tap, 16)] = part[:, v * SLICE : (v + 1) * SLICE].reshape(16, 16, SLICE)
        return carry

    if count == 1:
        tap_row(0, 0)
    else:
        lax.fori_loop(0, count, tap_row, 0)


def ring_add(*terms):
    total = terms[0].astype(F32)
    for term in terms[1:]:
        total = total + term.astype(F32)
    return total.astype(BF)


def step_kernel(
    clips_ref, cot_ref, gain_ref, bias_ref, w_hbm, f_ref, small_out,
    weights, lattice, slice_lattice, hidden_own, hidden_all, adj_own, full, slices, conv_out, conv_in, acc_y, acc_g, normed_s, inv_s,
    small_own, small_1, small_2, small_3, d_ref, slot_a, slot_b, from_left, from_right, stage_r, stage_l, mine, theirs,
    w_sems, own_sems, full_send, full_recv, slice_send, slice_recv, hid_send, hid_recv, y_send, y_recv,
    sends, recvs, keep_sems, s_sends, s_recvs,
):
    z, y, x, section, chan = coords()
    here = z * 8 + y * 2 + x

    def at_z(k):
        return k * 8 + y * 2 + x

    def at_y(k):
        return z * 8 + k * 2 + x

    barrier = pltpu.get_barrier_semaphore()

    def greet(dp, s, c):
        pl.semaphore_signal(barrier, inc=1, device_id={"dp": dp, "section": s, "chan": c}, device_id_type=MESH)

    for s in (0, 1):
        for c in (0, 1):
            for step in (1, 2, 3):
                greet(at_z((z + step) % 4), s, c)
                greet(at_y((y + step) % 4), s, c)
    greet(here, 1 - section, chan)
    greet(here, section, 1 - chan)
    greet(here, 1 - section, 1 - chan)
    greet(z * 8 + y * 2 + 1 - x, section, chan)

    def w_copy(t):
        return pltpu.make_async_copy(w_hbm.at[pl.ds(9 * t, 9)], weights.at[pl.ds(9 * t, 9)], w_sems.at[t])

    for t in (2, 1, 0):
        w_copy(t).start()

    def wait_weights(t):
        w_copy(t).wait()

    gain = column(gain_ref[...])
    bias = column(bias_ref[...])

    group = section * y + (1 - section) * z

    def ring(k):
        return section * at_y(k) + (1 - section) * at_z(k)

    def hidden_copy(step):
        return remote(
            hidden_own, hidden_all.at[:, pl.ds(pl.multiple_of(group * POS, POS), POS)],
            hid_send.at[step - 1], hid_recv.at[(4 - step) % 4], ring((group + step) % 4), section, chan,
        )

    def hidden_own_copy():
        return pltpu.make_async_copy(
            hidden_own, hidden_all.at[:, pl.ds(pl.multiple_of(group * POS, POS), POS)], own_sems.at[0]
        )

    def full_copy(c):
        return remote(adj_own, full.at[chan], full_send.at[c], full_recv.at[chan], here, 0, c)

    def cot_full_copy():
        return remote(adj_own, full.at[chan], full_send.at[0], full_recv.at[chan], here, 1, 1 - chan)

    def slice_copy(jj, c, dest_section):
        j = 2 * chan + jj
        slot = dest_section * y + (1 - dest_section) * z
        dp = dest_section * at_y(j) + (1 - dest_section) * at_z(j)
        return remote(
            adj_own.at[:, pl.ds(SLICE * jj, SLICE)], slices.at[slot], slice_send.at[2 * jj + c],
            slice_recv.at[slot], dp, dest_section, c,
        )

    def own_slice_copy():
        return pltpu.make_async_copy(
            adj_own.at[:, pl.ds(pl.multiple_of(y % 2 * SLICE, SLICE), SLICE)], slices.at[y], own_sems.at[1]
        )

    def conv_half(hh):
        return hh * chan + (1 - hh) * (1 - chan)

    def conv_copy(hh):
        return remote(conv_out.at[hh], conv_in.at[chan], y_send.at[hh], y_recv.at[chan], here, 1, conv_half(hh))

    zero_row = jnp.zeros((2, 4, 1, 16, 3 * CH), BF)
    lattice[:, :, 0:1] = zero_row
    lattice[:, :, 9:10] = zero_row
    zero_slice = jnp.zeros((4, 4, 1, 16, 3 * SLICE), BF)
    slice_lattice[:, :, 0:1] = zero_slice
    slice_lattice[:, :, 9:10] = zero_slice

    def fill(half, values):
        def store(v, moved):
            lattice[half, :, 1:9, :, v * CH : (v + 1) * CH] = moved.astype(BF).reshape(4, 8, 16, CH)

        shifted_columns(values, store)

    @pl.when(section == 0)
    def _():
        normed, shifted, inv_std = norm_forward(clips_ref[...].astype(F32), gain, bias)
        hidden_own[...] = silu(shifted).astype(BF).reshape(CH, POS)
        normed_s[...] = normed
        for f in range(4):
            inv_s[f] = jnp.broadcast_to(inv_std[f], (GROUP, 1, 128))

    @pl.when(section == 1)
    def _():
        adj_own[...] = cot_ref[...].astype(F32).T.astype(BF)

    pl.semaphore_wait(barrier, 28)

    @pl.when(section == 0)
    def _():
        for step in (1, 2, 3):
            hidden_copy(step).start()
        hidden_own_copy().start()
        fill(0, hidden_own[...].astype(F32).T)
        for hh in range(2):
            acc_y[...] = jnp.zeros_like(acc_y)
            start = pl.multiple_of(conv_half(hh) * CH, CH)
            conv_forward(lattice, weights, start, acc_y, wait_weights if hh == 0 else (lambda t: None))
            conv_out[hh] = acc_y[...].astype(BF)
            conv_copy(hh).start()

    @pl.when(section == 1)
    def _():
        cot_full_copy().start()
        for jj in range(2):
            for c in range(2):

                @pl.when((2 * chan + jj != y) | (chan != c))
                def _(jj=jj, c=c):
                    slice_copy(jj, c, 1).start()

        @pl.when(y // 2 == chan)
        def _():
            own_slice_copy().start()

        fill(chan, adj_own[...].astype(F32))
        acc_g[...] = jnp.zeros_like(acc_g)
        conv_transposed(lattice, weights, chan, acc_g, wait_weights)
        remote(adj_own, full.at[1 - chan], full_send.at[0], full_recv.at[1 - chan], here, 1, 1 - chan).wait_recv()
        fill(1 - chan, full[1 - chan].astype(F32))
        conv_transposed(lattice, weights, 1 - chan, acc_g, lambda t: None)
        for c in range(2):
            remote(conv_out.at[c], conv_in.at[c], y_send.at[c], y_recv.at[c], here, 1, c).wait_recv()
        summed = conv_in[0].astype(F32) + conv_in[1].astype(F32)
        act = (clips_ref[...].astype(F32) + summed.T).astype(BF).astype(F32)
        normed, shifted, inv_std = norm_forward(act, gain, bias)
        hidden_own[...] = silu(shifted).astype(BF).reshape(CH, POS)
        for step in (1, 2, 3):
            hidden_copy(step).start()
        hidden_own_copy().start()
        grad_normed, gain_term, bias_term = norm_backward(acc_g[...], normed, shifted, inv_std, gain)
        small_own[...] = small_rows(gain_term, bias_term)
        grad_act = norm_input_grad(grad_normed, normed, inv_std).reshape(CH, POS)
        adjoint = (cot_ref[...].astype(F32) + grad_act).T.astype(BF)
        cot_full_copy().wait_send()
        for jj in range(2):
            for c in range(2):

                @pl.when((2 * chan + jj != y) | (chan != c))
                def _(jj=jj, c=c):
                    slice_copy(jj, c, 1).wait_send()

        @pl.when(y // 2 == chan)
        def _():
            own_slice_copy().wait()

        adj_own[...] = adjoint
        for jj in range(2):
            for c in range(2):
                slice_copy(jj, c, 0).start()
        for c in range(2):
            full_copy(c).start()
        for k in range(4):

            @pl.when((k != y) | (y // 2 != chan))
            def _(k=k):
                remote(
                    adj_own.at[:, pl.ds(0, SLICE)], slices.at[k], slice_send.at[0], slice_recv.at[k], here, 1, 1 - chan
                ).wait_recv()

    @pl.when(section == 0)
    def _():
        for k in range(4):
            remote(
                adj_own.at[:, pl.ds(0, SLICE)], slices.at[k], slice_send.at[0], slice_recv.at[k], here, 1, chan
            ).wait_recv()

    for k in range(4):

        def store(v, moved, k=k):
            slice_lattice[k, :, 1:9, :, v * SLICE : (v + 1) * SLICE] = moved.astype(BF).reshape(4, 8, 16, SLICE)

        shifted_columns(slices[k].astype(F32), store)
    hidden_own_copy().wait()
    for step in (1, 2, 3):
        came = (group + step) % 4
        remote(
            hidden_own, hidden_all.at[:, pl.ds(pl.multiple_of(came * POS, POS), POS)],
            hid_send.at[step - 1], hid_recv.at[step], ring((group + step) % 4), section, chan,
        ).wait_recv()

    turn = section * z + (1 - section) * y

    def along(step):
        return section * at_z((z + step) % 4) + (1 - section) * at_y((y + step) % 4)

    def across(step):
        return section * at_y((y + step) % 4) + (1 - section) * at_z((z + step) % 4)

    right, left, opp = along(1), along(3), along(2)
    up, down, far = across(1), across(3), across(2)
    pair = z * 8 + y * 2 + 1 - x
    started = []

    class Chunk:
        def __init__(self, n):
            before = sum(c[0] for c in CHUNKS[:n])
            self.n, self.copies, self.here = n, {}, set()
            self.units, self.split = CHUNKS[n]
            self.base = UNITS - before - self.units
            self.blk, self.hlf = self.units // 4, self.units // 8
            self.eighth = pl.ds(before // 8, self.hlf)
            self.quarter = pl.ds(before // 4, self.blk)
            self.halves = (pl.ds(before // 4, self.hlf), pl.ds(before // 4 + self.hlf, self.hlf))

        def send(self, key, src, dst, dp):
            k = len(self.copies)
            copy = remote(src, dst, sends.at[self.n, k], recvs.at[self.n, k], dp, section, chan)
            copy.start()
            self.copies[key] = copy
            started.append(copy)

        def arrive(self, *keys):
            for key in keys:
                if key not in self.here:
                    self.here.add(key)
                    self.copies[key].wait_recv()

        def half(self, k, h):
            place = (turn + k) % 4
            if self.split:
                return pl.ds(self.base + h * (self.units // 2) + place * self.hlf, self.hlf)
            return pl.ds(self.base + place * self.blk + h * self.hlf, self.hlf)

        def block(self, k):
            return self.half(k, x) if self.split else pl.ds(self.base + (turn + k) % 4 * self.blk, self.blk)

        def part(self, k, h):
            if self.split:
                start = self.base + x * (self.units // 2) + (turn + k) % 4 * self.hlf
                return pl.ds(start + h * (self.hlf // 2), self.hlf // 2)
            return self.half(k, h)

        def slab(self, j, where):
            return f_ref.at[(group + j) % 4, where]

        def same(self, key, ref, dp):
            self.send(key, ref, ref, dp)

        def rs(self):
            self.send("ra", d_ref.at[self.half(2, 0)], slot_a.at[self.eighth], right)
            self.send("rb", d_ref.at[self.half(2, 1)], slot_b.at[self.eighth], left)
            self.send("r1", d_ref.at[self.half(1, 1)], from_left.at[self.halves[1]], right)
            self.send("l0", d_ref.at[self.half(3, 0)], from_right.at[self.halves[0]], left)

        def rh1(self):
            self.arrive("ra")
            stage_r[self.eighth] = ring_add(d_ref[self.half(1, 0)], slot_a[self.eighth])
            self.send("r0", stage_r.at[self.eighth], from_left.at[self.halves[0]], right)

        def rh2(self):
            self.arrive("rb")
            stage_l[self.eighth] = ring_add(d_ref[self.half(3, 1)], slot_b[self.eighth])
            self.send("l1", stage_l.at[self.eighth], from_right.at[self.halves[1]], left)

        def other(self):
            return pl.ds(self.halves[0].start + (1 - x) * self.hlf, self.hlf)

        def own(self):
            return pl.ds(self.halves[0].start + x * self.hlf, self.hlf)

        def re(self):
            self.arrive("r1", "l0", "r0", "l1")
            for h, where in enumerate(self.halves):
                mine[0, where] = ring_add(d_ref[self.half(0, h)], from_left[where], from_right[where])
            if self.split:
                self.send("p", mine.at[0, self.other()], theirs.at[self.halves[0]], pair)
            else:
                self.send("p", mine.at[0, self.quarter], theirs.at[self.quarter], pair)

        def final(self):
            return mine.at[1, self.halves[0] if self.split else self.quarter]

        def keep(self):
            return pltpu.make_async_copy(self.final(), self.slab(0, self.block(0)), keep_sems.at[self.n])

        def gs(self):
            self.arrive("p")
            if self.split:
                mine[1, self.halves[0]] = ring_add(mine[0, self.own()], theirs[self.halves[0]])
            else:
                mine[1, self.quarter] = ring_add(mine[0, self.quarter], theirs[self.quarter])
            to = self.slab(0, self.block(0))
            self.send("gr", self.final(), to, right)
            self.send("gl", self.final(), to, left)
            self.send("u0", self.final(), to, up)
            self.send("d0", self.final(), to, down)
            self.keep().start()

        def h1(self):
            self.arrive("gr")
            self.same("hr", self.slab(0, self.part(3, 0)), right)

        def h2(self):
            self.arrive("gl")
            self.same("hl", self.slab(0, self.part(1, 1)), left)

        def s(self, k):
            self.arrive(*{1: ("gl",), 2: ("hr", "hl"), 3: ("gr",)}[k])
            self.same(f"u{k}", self.slab(0, self.block(k)), up)
            self.same(f"d{k}", self.slab(0, self.block(k)), down)

        def pu(self, k):
            self.arrive(f"u{k}")
            self.same(f"uu{k}", self.slab(3, self.part(k, 0)), up)

        def pd(self, k):
            self.arrive(f"d{k}")
            self.same(f"dd{k}", self.slab(1, self.part(k, 1)), down)

        def x(self, j):
            if j == 0:
                self.arrive("gr", "gl", "hr", "hl")
                self.keep().wait()
            elif j == 3:
                self.arrive("u0", "u1", "u2", "u3")
            elif j == 1:
                self.arrive("d0", "d1", "d2", "d3")
            else:
                self.arrive(*(f"{d}{k}" for d in ("uu", "dd") for k in range(4)))
            self.same(f"x{j}", self.slab(j, pl.ds(self.base + x * (self.units // 2), self.units // 2)), pair)

        def end(self):
            self.arrive(*self.copies)
            if not self.split:
                self.keep().wait()

    def small_copies(buf, peers, slot, base, src):
        buf[slot] = src[...]
        copies = []
        for k, dp in enumerate(peers):
            copies.append(remote(src, buf.at[slot], s_sends.at[base + k], s_recvs.at[base + k], dp, section, chan))
        for copy in copies:
            copy.start()
        return copies

    chunks = [Chunk(n) for n in range(len(CHUNKS))]

    weight_gradient(hidden_all, slice_lattice, d_ref, 2, 2, 1)
    weight_gradient(hidden_all, slice_lattice, d_ref, 2, 1, 1)
    chunks[0].rs()
    chunks[1].rs()
    weight_gradient(hidden_all, slice_lattice, d_ref, 2, 0, 1)
    weight_gradient(hidden_all, slice_lattice, d_ref, 1, 2, 1)
    weight_gradient(hidden_all, slice_lattice, d_ref, 1, 1, 2)
    chunks[2].rs()
    chunks[0].rh1()
    chunks[0].rh2()
    weight_gradient(hidden_all, slice_lattice, d_ref, 0, 2, 3)
    chunks[3].rs()
    chunks[1].rh1()
    chunks[1].rh2()
    chunks[4].rs()
    chunks[0].re()
    chunks[2].rh2()
    chunks[2].rh1()
    chunks[1].re()
    chunks[3].rh1()
    chunks[3].rh2()
    chunks[0].gs()
    @pl.when(section == 0)
    def _():
        for k in range(2):
            remote(adj_own, full.at[k], full_send.at[k], full_recv.at[k], here, 1, chan).wait_recv()
            fill(k, full[k].astype(F32))
        acc_g[...] = jnp.zeros_like(acc_g)

    chunks[4].rh1()
    chunks[4].rh2()
    chunks[2].re()
    chunks[1].gs()
    chunks[3].re()
    @pl.when(section == 0)
    def _():
        conv_transposed(lattice, weights, 0, acc_g, lambda t: None, (2,))

    chunks[0].h1()
    chunks[0].h2()
    chunks[0].s(3)
    chunks[0].s(1)
    chunks[0].pu(0)
    chunks[0].pd(0)
    @pl.when(section == 0)
    def _():
        conv_transposed(lattice, weights, 1, acc_g, lambda t: None, (2,))

    chunks[4].re()
    chunks[2].gs()
    chunks[1].h1()
    chunks[1].h2()
    chunks[1].s(3)
    @pl.when(section == 0)
    def _():
        conv_transposed(lattice, weights, 0, acc_g, lambda t: None, (1,))

    chunks[1].s(1)
    chunks[0].s(2)
    chunks[0].x(0)
    chunks[1].pu(0)
    chunks[1].pd(0)
    chunks[0].pu(3)
    chunks[0].pd(3)
    chunks[0].pu(1)
    chunks[0].pd(1)
    @pl.when(section == 0)
    def _():
        conv_transposed(lattice, weights, 1, acc_g, lambda t: None, (1,))

    chunks[3].gs()
    @pl.when(section == 0)
    def _():
        conv_transposed(lattice, weights, 0, acc_g, lambda t: None, (0,))

    chunks[1].s(2)
    chunks[2].h2()
    chunks[2].s(1)
    chunks[0].pu(2)
    chunks[0].pd(2)
    @pl.when(section == 0)
    def _():
        conv_transposed(lattice, weights, 1, acc_g, lambda t: None, (0,))

    chunks[0].x(3)
    chunks[0].x(1)
    chunks[2].h1()
    chunks[2].s(3)
    chunks[2].pu(0)
    chunks[2].pd(0)
    chunks[1].pd(3)
    chunks[1].pu(3)
    chunks[1].pu(1)
    chunks[1].pd(1)
    @pl.when(section == 0)
    def _():
        normed = normed_s[...]
        shifted = jnp.concatenate([normed[:, :, 128 * f : 128 * f + 128] * gain + bias for f in range(4)], axis=2)
        inv_std = [inv_s[f] for f in range(4)]
        unused, gain_term, bias_term = norm_backward(acc_g[...], normed, shifted, inv_std, gain)
        small_own[...] = small_rows(gain_term, bias_term)

    chunks[4].gs()
    chunks[0].x(2)
    first = small_copies(small_1, (right, opp, left), turn, 0, small_own)
    chunks[3].h1()
    chunks[3].s(3)
    chunks[1].pu(2)
    chunks[1].pd(2)
    chunks[2].s(2)
    chunks[2].x(0)
    chunks[3].h2()
    chunks[3].s(1)
    chunks[3].pu(0)
    chunks[3].pd(0)
    chunks[2].pu(1)
    chunks[2].pd(1)
    chunks[2].pu(3)
    chunks[2].pd(3)
    for copy in first:
        copy.wait()
    small_2[4] = small_1[0] + small_1[1] + small_1[2] + small_1[3]
    second = small_copies(small_2, (up, far, down), group, 3, small_2.at[4])
    chunks[2].pu(2)
    chunks[2].pd(2)
    chunks[2].x(3)
    chunks[2].x(1)
    chunks[3].s(2)
    chunks[4].h2()
    chunks[4].h1()
    chunks[4].s(3)
    chunks[4].s(1)
    chunks[3].pu(3)
    chunks[3].pd(3)
    chunks[3].pu(1)
    chunks[3].pd(1)
    chunks[4].pu(0)
    chunks[4].pd(0)
    chunks[2].x(2)
    chunks[3].pu(2)
    chunks[3].pd(2)
    for copy in second:
        copy.wait()
    small_3[0] = small_2[0] + small_2[1] + small_2[2] + small_2[3]
    third = remote(small_3.at[0], small_3.at[1], s_sends.at[6], s_recvs.at[6], pair, section, chan)
    third.start()
    chunks[4].s(2)
    chunks[4].pd(3)
    chunks[4].pu(3)
    chunks[4].pd(1)
    chunks[4].pu(1)
    chunks[4].pd(2)
    chunks[4].pu(2)
    for chunk in chunks:
        chunk.end()
    third.wait()
    small_out[...] = small_3[0] + small_3[1]

    @pl.when(section == 0)
    def _():
        for hh in range(2):
            conv_copy(hh).wait_send()

    @pl.when(section == 1)
    def _():
        for jj in range(2):
            for k in range(2):
                slice_copy(jj, k, 0).wait_send()
        for k in range(2):
            full_copy(k).wait_send()

    for step in (1, 2, 3):
        hidden_copy(step).wait_send()
    for copy in started:
        copy.wait_send()


def step(clips, cot, gain, bias, weights):
    vmem = pl.BlockSpec(memory_space=pltpu.VMEM)
    dma = pltpu.SemaphoreType.DMA
    return pl.pallas_call(
        step_kernel,
        out_shape=(pltpu.VMEM((4, UNITS, 16, SLICE), BF), pltpu.VMEM((8, CH), F32)),
        in_specs=[vmem, vmem, vmem, vmem, pl.BlockSpec(memory_space=pl.ANY)],
        out_specs=(vmem, vmem),
        scratch_shapes=[
            pltpu.VMEM((27, CH, FULL), BF),
            pltpu.VMEM((2, 4, 10, 16, 3 * CH), BF),
            pltpu.VMEM((4, 4, 10, 16, 3 * SLICE), BF),
            pltpu.VMEM((CH, POS), BF),
            pltpu.VMEM((CH, 4 * POS), BF),
            pltpu.VMEM((POS, CH), BF),
            pltpu.VMEM((2, POS, CH), BF),
            pltpu.VMEM((4, POS, SLICE), BF),
            pltpu.VMEM((2, POS, CH), BF),
            pltpu.VMEM((2, POS, CH), BF),
            pltpu.VMEM((POS, CH), F32),
            pltpu.VMEM((CH, POS), F32),
            pltpu.VMEM((GROUP, GROUP, POS), F32),
            pltpu.VMEM((4, GROUP, 1, 128), F32),
            pltpu.VMEM((8, CH), F32),
            pltpu.VMEM((4, 8, CH), F32),
            pltpu.VMEM((5, 8, CH), F32),
            pltpu.VMEM((2, 8, CH), F32),
            pltpu.VMEM((UNITS, 16, SLICE), BF),
            pltpu.VMEM((UNITS // 8, 16, SLICE), BF),
            pltpu.VMEM((UNITS // 8, 16, SLICE), BF),
            pltpu.VMEM((UNITS // 4, 16, SLICE), BF),
            pltpu.VMEM((UNITS // 4, 16, SLICE), BF),
            pltpu.VMEM((UNITS // 8, 16, SLICE), BF),
            pltpu.VMEM((UNITS // 8, 16, SLICE), BF),
            pltpu.VMEM((2, UNITS // 4, 16, SLICE), BF),
            pltpu.VMEM((UNITS // 4, 16, SLICE), BF),
            dma((3,)), dma((2,)), dma((2,)), dma((2,)), dma((4,)), dma((4,)), dma((3,)), dma((4,)), dma((2,)), dma((2,)),
            dma((len(CHUNKS), 32)), dma((len(CHUNKS), 32)), dma((len(CHUNKS),)), dma((7,)), dma((7,)),
        ],
        compiler_params=pltpu.CompilerParams(collective_id=1, has_side_effects=True, vmem_limit_bytes=48 << 20),
        name="step",
    )(clips, cot, gain, bias, weights)


def widen_kernel(slabs, sums, out, gain_out, bias_out, rows_a, rows_b, sems):
    steps, units = WIDEN, UNITS // WIDEN
    rows = units * 16
    gain_out[...] = sums[0:1]
    bias_out[...] = sums[1:2]
    buffers = (rows_a, rows_b)

    def copy(i):
        return pltpu.make_async_copy(buffers[i % 2], out.at[pl.ds(i * rows, rows)], sems.at[i % 2])

    for i in range(steps):
        if i >= 2:
            copy(i - 2).wait()
        for k in range(4):
            buffers[i % 2][:, k * SLICE : (k + 1) * SLICE] = slabs[k, i * units : (i + 1) * units].reshape(rows, SLICE).astype(F32)
        copy(i).start()
    copy(steps - 2).wait()
    copy(steps - 1).wait()


def widen(slabs, sums):
    vmem = pl.BlockSpec(memory_space=pltpu.VMEM)
    rows = UNITS // WIDEN * 16
    return pl.pallas_call(
        widen_kernel,
        out_shape=(
            jax.ShapeDtypeStruct((UNITS * 16, FULL), F32),
            jax.ShapeDtypeStruct((1, CH), F32),
            jax.ShapeDtypeStruct((1, CH), F32),
        ),
        in_specs=[vmem, vmem],
        out_specs=(pl.BlockSpec(memory_space=pl.ANY), vmem, vmem),
        scratch_shapes=[pltpu.VMEM((rows, FULL), F32), pltpu.VMEM((rows, FULL), F32), pltpu.SemaphoreType.DMA((2,))],
        compiler_params=pltpu.CompilerParams(vmem_limit_bytes=20 << 20),
        name="widen",
    )(slabs, sums)


def shards(clips, conv_weight, norm_gain, norm_bias, cotangent):
    slabs, sums = step(clips.reshape(CH, POS), cotangent.reshape(CH, POS), norm_gain, norm_bias, conv_weight[0])
    weight_grad, gain_grad, bias_grad = widen(slabs, sums)
    return weight_grad.reshape(1, 27, CH, FULL), gain_grad, bias_grad


def solution(mesh):
    in_specs = (
        P("dp", "chan", None, None),
        P("section", None, "chan", None),
        P("section", "chan"),
        P("section", "chan"),
        P("dp", "chan", None, None),
    )
    out_specs = (P("section", None, "chan", None), P("section", "chan"), P("section", "chan"))
    return jax.shard_map(shards, mesh=mesh, in_specs=in_specs, out_specs=out_specs, check_vma=False)
```

```python
import jax
import jax.numpy as jnp
from jax import lax
from jax.experimental import pallas as pl
from jax.experimental.pallas import tpu as pltpu
from jax.sharding import PartitionSpec as P

EPSILON = 1e-05
MESH = pl.DeviceIdType.MESH
BF = jnp.bfloat16
F32 = jnp.float32

CH = 256
FULL = 512
POS = 512
SLICE = 128
GROUP = 16
UNITS = 432
CHUNKS = ((48, True), (48, False), (96, True), (96, False), (144, False))
WIDEN = 27
SLOTS = 6


def coords():
    dp = lax.axis_index("dp")
    return dp // 8, dp // 2 % 4, dp % 2, lax.axis_index("section"), lax.axis_index("chan")


def remote(src, dst, send_sem, recv_sem, dp, section, chan):
    return pltpu.make_async_remote_copy(
        src_ref=src,
        dst_ref=dst,
        send_sem=send_sem,
        recv_sem=recv_sem,
        device_id={"dp": dp, "section": section, "chan": chan},
        device_id_type=MESH,
    )


def norm_frame(values):
    scale = 1.0 / (GROUP * 128)
    centre = jnp.sum(values, axis=(1, 2), keepdims=True) * scale
    moved = values - centre
    spread = jnp.sum(moved * moved, axis=(1, 2), keepdims=True) * scale
    inv_std = lax.rsqrt(spread + EPSILON)
    return moved * inv_std, inv_std


def silu(shifted):
    return shifted * (1.0 / (1.0 + jnp.exp(-shifted)))


def norm_forward(act, gain, bias):
    normed, inv_std = norm_frame(act.reshape(GROUP, GROUP, 128))
    return normed, normed * gain + bias, inv_std


def norm_backward(grad_hidden, normed, shifted, gain):
    sig = 1.0 / (1.0 + jnp.exp(-shifted))
    grad_shift = grad_hidden.reshape(GROUP, GROUP, 128) * sig * (1.0 + shifted * (1.0 - sig))
    gain_term = jnp.sum(grad_shift * normed, axis=2, keepdims=True)
    bias_term = jnp.sum(grad_shift, axis=2, keepdims=True)
    return grad_shift * gain, gain_term, bias_term


def norm_input_grad(grad_normed, normed, inv_std):
    scale = 1.0 / (GROUP * 128)
    mean_grad = jnp.sum(grad_normed, axis=(1, 2), keepdims=True) * scale
    mean_cross = jnp.sum(grad_normed * normed, axis=(1, 2), keepdims=True) * scale
    return (grad_normed - mean_grad - normed * mean_cross) * inv_std


def small_rows(gain_term, bias_term):
    lane = lax.broadcasted_iota(jnp.int32, (CH, 128), 1)
    gain_col = jnp.broadcast_to(gain_term.reshape(CH, 1), (CH, 128))
    bias_col = jnp.broadcast_to(bias_term.reshape(CH, 1), (CH, 128))
    both = jnp.where(lane == 0, gain_col, jnp.where(lane == 1, bias_col, 0.0))
    return both.T[:8]


def shifted_columns(values, store):
    col = lax.broadcasted_iota(jnp.int32, values.shape, 0) % 16
    store(0, jnp.where(col == 0, 0.0, pltpu.roll(values, 1, 0)))
    store(1, values)
    store(2, jnp.where(col == 15, 0.0, pltpu.roll(values, POS - 1, 0)))


def column(row):
    return jnp.broadcast_to(row, (128, CH)).T.reshape(GROUP, GROUP, 128)


def conv_forward(lattice, weights, start, pair, acc, wait_weights):
    for t in (2, 1, 0)[: 2 + pair]:
        wait_weights(t)
        frame_in = max(2 * pair + t - 2, 0)
        frame_out = frame_in + 2 - t
        count = 2 * pair + 2 - frame_out
        rows = 128 * count

        def tap_row(r, carry, t=t, frame_in=frame_in, frame_out=frame_out, count=count, rows=rows):
            lhs = lattice[0, frame_in : frame_in + count, pl.ds(r, 8)].reshape(rows, 3 * CH)
            rhs = weights[pl.ds(9 * t + 3 * r, 3), :, pl.ds(start, CH)].reshape(3 * CH, CH)
            part = jnp.dot(lhs, rhs, preferred_element_type=F32)
            acc[pl.ds(128 * frame_out, rows)] = acc[pl.ds(128 * frame_out, rows)] + part
            return carry

        lax.fori_loop(0, 3, tap_row, 0)


def conv_transposed(lattice, weights, half, acc, wait_weights, steps=(2, 1, 0)):
    start = pl.multiple_of(half * CH, CH)
    for t in steps:
        wait_weights(t)
        cols = 128 * (t + 2)

        def tap_row(r, carry, t=t, cols=cols):
            part = None
            for v in range(3):
                rhs = lattice[half, 2 - t : 4, pl.ds(2 - r, 8), :, v * CH : (v + 1) * CH].reshape(cols, CH)
                one = lax.dot_general(
                    weights[9 * t + 3 * r + 2 - v, :, pl.ds(start, CH)], rhs, (((1,), (1,)), ((), ())),
                    preferred_element_type=F32,
                )
                part = one if part is None else part + one
            acc[:, 0:cols] = acc[:, 0:cols] + part
            return carry

        lax.fori_loop(0, 3, tap_row, 0)


def weight_gradient(hidden_all, lattice, out, t, first, count):
    cols = 128 * (t + 2)
    lhs = jnp.concatenate([hidden_all[:, POS * k : POS * k + cols] for k in range(4)], axis=1)

    def tap_row(step, carry):
        r = first - step
        rhs = lattice[:, 2 - t : 4, pl.ds(2 - r, 8)].reshape(4 * cols, 3 * SLICE)
        part = jnp.dot(lhs, rhs, preferred_element_type=F32).astype(BF)
        for v in range(3):
            tap = 9 * t + 3 * r + 2 - v
            out[pl.ds(16 * tap, 16)] = part[:, v * SLICE : (v + 1) * SLICE].reshape(16, 16, SLICE)
        return carry

    if count == 1:
        tap_row(0, 0)
    else:
        lax.fori_loop(0, count, tap_row, 0)


def ring_add(*terms):
    total = terms[0].astype(F32)
    for term in terms[1:]:
        total = total + term.astype(F32)
    return total.astype(BF)


def step_kernel(
    clips_ref, cot_ref, gain_ref, bias_ref, w_hbm, f_ref, small_out,
    weights, lattice, slice_lattice, hidden_own, hidden_all, adj_own, full, slices, conv_out, conv_in, acc_y, acc_g, normed_s, raw, raw_cot, adj_new,
    small_own, small_1, small_2, small_3, d_ref, slot_a, slot_b, from_left, from_right, stage_r, stage_l, mine, theirs,
    w_sems, own_sems, full_send, full_recv, slice_send, slice_recv, adj_send, adj_recv, hid_send, hid_recv, y_send, y_recv,
    sends, recvs, keep_sems, s_sends, s_recvs,
):
    z, y, x, section, chan = coords()
    here = z * 8 + y * 2 + x

    def at_z(k):
        return k * 8 + y * 2 + x

    def at_y(k):
        return z * 8 + k * 2 + x

    barrier = pltpu.get_barrier_semaphore()

    def w_copy(t):
        return pltpu.make_async_copy(w_hbm.at[pl.ds(9 * t, 9)], weights.at[pl.ds(9 * t, 9)], w_sems.at[t])

    for t in (2, 1, 0):
        w_copy(t).start()

    def greet(dp, s, c):
        pl.semaphore_signal(barrier, inc=1, device_id={"dp": dp, "section": s, "chan": c}, device_id_type=MESH)

    for s in (0, 1):
        for c in (0, 1):
            for step in (1, 2, 3):
                greet(at_z((z + step) % 4), s, c)
                greet(at_y((y + step) % 4), s, c)
    greet(here, 1 - section, chan)
    greet(here, section, 1 - chan)
    greet(here, 1 - section, 1 - chan)
    greet(z * 8 + y * 2 + 1 - x, section, chan)

    def wait_weights(t):
        w_copy(t).wait()

    gain = column(gain_ref[...])
    bias = column(bias_ref[...])

    group = section * y + (1 - section) * z

    def ring(k):
        return section * at_y(k) + (1 - section) * at_z(k)

    def frames(pair, at):
        return pl.ds(pl.multiple_of(at * POS + 256 * pair, 256), 256)

    def hidden_copy(step, pair):
        return remote(
            hidden_own.at[:, pl.ds(256 * pair, 256)], hidden_all.at[:, frames(pair, group)],
            hid_send.at[pair, step - 1], hid_recv.at[pair, (4 - step) % 4], ring((group + step) % 4), section, chan,
        )

    def hidden_arrival(step, pair):
        return remote(
            hidden_own.at[:, pl.ds(256 * pair, 256)], hidden_all.at[:, frames(pair, (group + step) % 4)],
            hid_send.at[pair, step - 1], hid_recv.at[pair, step], ring((group + step) % 4), section, chan,
        )

    def hidden_own_copy():
        return pltpu.make_async_copy(
            hidden_own, hidden_all.at[:, pl.ds(pl.multiple_of(group * POS, POS), POS)], own_sems.at[0]
        )

    def full_copy(c):
        return remote(adj_new, full.at[chan], full_send.at[c], full_recv.at[chan], here, 0, c)

    def cot_full_copy():
        return remote(adj_own, full.at[chan], full_send.at[0], full_recv.at[chan], here, 1, 1 - chan)

    def cot_slice_copy(jj, c):
        return remote(
            adj_own.at[:, pl.ds(SLICE * jj, SLICE)], slices.at[y], slice_send.at[2 * jj + c], slice_recv.at[y],
            at_y(2 * chan + jj), 1, c,
        )

    def adj_slice_copy(jj, c, pair):
        rows = pl.ds(256 * pair, 256)
        return remote(
            adj_new.at[rows, pl.ds(SLICE * jj, SLICE)], slices.at[z, rows], adj_send.at[pair, 2 * jj + c],
            adj_recv.at[pair, z], at_z(2 * chan + jj), 0, c,
        )

    def own_slice_copy():
        return pltpu.make_async_copy(
            adj_own.at[:, pl.ds(pl.multiple_of(y % 2 * SLICE, SLICE), SLICE)], slices.at[y], own_sems.at[1]
        )

    def conv_half(hh):
        return hh * chan + (1 - hh) * (1 - chan)

    def conv_copy(hh, pair):
        rows = pl.ds(256 * pair, 256)
        return remote(
            conv_out.at[hh, rows], conv_in.at[chan, rows], y_send.at[pair, hh], y_recv.at[pair, chan], here, 1, conv_half(hh)
        )

    def conv_arrival(c, pair):
        rows = pl.ds(256 * pair, 256)
        return remote(conv_out.at[c, rows], conv_in.at[c, rows], y_send.at[pair, c], y_recv.at[pair, c], here, 1, c)

    def frame(buffer, f):
        return buffer[pl.ds(f, CH, stride=4), :]

    zero_row = jnp.zeros((2, 4, 1, 16, 3 * CH), BF)
    lattice[:, :, 0:1] = zero_row
    lattice[:, :, 9:10] = zero_row
    zero_slice = jnp.zeros((4, 4, 1, 16, 3 * SLICE), BF)
    slice_lattice[:, :, 0:1] = zero_slice
    slice_lattice[:, :, 9:10] = zero_slice

    def fill(half, values):
        def store(v, moved):
            lattice[half, :, 1:9, :, v * CH : (v + 1) * CH] = moved.astype(BF).reshape(4, 8, 16, CH)

        shifted_columns(values, store)

    raw[...] = clips_ref[...].astype(F32)

    @pl.when(section == 0)
    def _():
        for f in range(4):
            lanes = slice(128 * f, 128 * f + 128)
            normed, shifted, inv_std = norm_forward(frame(raw, f), gain, bias)
            hidden_own[:, lanes] = silu(shifted).astype(BF).reshape(CH, 128)
            normed_s[:, :, lanes] = normed

    @pl.when(section == 1)
    def _():
        raw_cot[...] = cot_ref[...].astype(F32)
        for f in range(4):
            adj_own[128 * f : 128 * f + 128] = frame(raw_cot, f).T.astype(BF)

    pl.semaphore_wait(barrier, 28)

    @pl.when(section == 0)
    def _():
        for pair in range(2):
            for step in (1, 2, 3):
                hidden_copy(step, pair).start()
        hidden_own_copy().start()
        fill(0, hidden_own[...].astype(F32).T)
        for pair in range(2):
            for hh in range(2):
                rows = slice(256 * pair, 256 * pair + 256)
                acc_y[rows] = jnp.zeros((256, CH), F32)
                start = pl.multiple_of(conv_half(hh) * CH, CH)

                def first_use(t, pair=pair, hh=hh):
                    if hh == 0 and (t == 0) == (pair == 1):
                        wait_weights(t)

                conv_forward(lattice, weights, start, pair, acc_y, first_use)
                conv_out[hh, rows] = acc_y[rows].astype(BF)
                conv_copy(hh, pair).start()

    @pl.when(section == 1)
    def _():
        cot_full_copy().start()
        for jj in range(2):
            for c in range(2):

                @pl.when((2 * chan + jj != y) | (chan != c))
                def _(jj=jj, c=c):
                    cot_slice_copy(jj, c).start()

        @pl.when(y // 2 == chan)
        def _():
            own_slice_copy().start()

        fill(chan, adj_own[...].astype(F32))
        acc_g[...] = jnp.zeros_like(acc_g)
        conv_transposed(lattice, weights, chan, acc_g, wait_weights)
        remote(adj_own, full.at[1 - chan], full_send.at[0], full_recv.at[1 - chan], here, 1, 1 - chan).wait_recv()
        fill(1 - chan, full[1 - chan].astype(F32))
        conv_transposed(lattice, weights, 1 - chan, acc_g, lambda t: None)
        gain_sum, bias_sum = None, None
        for pair in range(2):
            for c in range(2):
                conv_arrival(c, pair).wait_recv()
            saved = []
            for f in (2 * pair, 2 * pair + 1):
                rows = slice(128 * f, 128 * f + 128)
                summed = conv_in[0, rows].astype(F32) + conv_in[1, rows].astype(F32)
                act = (frame(raw, f) + summed.T).astype(BF).astype(F32)
                parts = norm_forward(act, gain, bias)
                hidden_own[:, rows] = silu(parts[1]).astype(BF).reshape(CH, 128)
                saved.append((f, rows, parts))
            for step in (1, 2, 3):
                hidden_copy(step, pair).start()
            for f, rows, (normed, shifted, inv_std) in saved:
                grad_normed, gain_term, bias_term = norm_backward(acc_g[:, rows], normed, shifted, gain)
                grad_act = norm_input_grad(grad_normed, normed, inv_std).reshape(CH, 128)
                adj_new[rows] = (frame(raw_cot, f) + grad_act).T.astype(BF)
                gain_sum = gain_term if gain_sum is None else gain_sum + gain_term
                bias_sum = bias_term if bias_sum is None else bias_sum + bias_term
            for jj in range(2):
                for c in range(2):
                    adj_slice_copy(jj, c, pair).start()
        hidden_own_copy().start()
        for c in range(2):
            if c == 0:
                cot_full_copy().wait_send()
            full_copy(c).start()
        small_own[...] = small_rows(gain_sum, bias_sum)
        for k in range(4):

            @pl.when((k != y) | (y // 2 != chan))
            def _(k=k):
                remote(
                    adj_own.at[:, pl.ds(0, SLICE)], slices.at[k], slice_send.at[0], slice_recv.at[k], here, 1, 1 - chan
                ).wait_recv()

        @pl.when(y // 2 == chan)
        def _():
            own_slice_copy().wait()

    @pl.when(section == 0)
    def _():
        for k in range(4):
            for pair in range(2):
                rows = pl.ds(256 * pair, 256)
                remote(
                    adj_new.at[rows, pl.ds(0, SLICE)], slices.at[k, rows], adj_send.at[pair, 0], adj_recv.at[pair, k],
                    here, 1, chan,
                ).wait_recv()

    for k in range(4):

        def store(v, moved, k=k):
            slice_lattice[k, :, 1:9, :, v * SLICE : (v + 1) * SLICE] = moved.astype(BF).reshape(4, 8, 16, SLICE)

        shifted_columns(slices[k].astype(F32), store)
    hidden_own_copy().wait()
    for pair in range(2):
        for step in (1, 2, 3):
            hidden_arrival(step, pair).wait_recv()

    turn = section * z + (1 - section) * y

    def along(step):
        return section * at_z((z + step) % 4) + (1 - section) * at_y((y + step) % 4)

    def across(step):
        return section * at_y((y + step) % 4) + (1 - section) * at_z((z + step) % 4)

    right, left, opp = along(1), along(3), along(2)
    up, down, far = across(1), across(3), across(2)
    pair = z * 8 + y * 2 + 1 - x
    started = []

    class Chunk:
        def __init__(self, n):
            before = sum(c[0] for c in CHUNKS[:n])
            self.n, self.copies, self.here = n, {}, set()
            self.units, self.split = CHUNKS[n]
            self.base = UNITS - before - self.units
            self.blk, self.hlf = self.units // 4, self.units // 8
            self.eighth = pl.ds(before // 8, self.hlf)
            self.quarter = pl.ds(before // 4, self.blk)
            self.halves = (pl.ds(before // 4, self.hlf), pl.ds(before // 4 + self.hlf, self.hlf))

        def send(self, key, src, dst, dp):
            k = len(self.copies)
            copy = remote(src, dst, sends.at[self.n, k], recvs.at[self.n, k], dp, section, chan)
            copy.start()
            self.copies[key] = copy
            started.append(copy)

        def arrive(self, *keys):
            for key in keys:
                if key not in self.here:
                    self.here.add(key)
                    self.copies[key].wait_recv()

        def half(self, k, h):
            place = (turn + k) % 4
            if self.split:
                return pl.ds(self.base + h * (self.units // 2) + place * self.hlf, self.hlf)
            return pl.ds(self.base + place * self.blk + h * self.hlf, self.hlf)

        def block(self, k):
            return self.half(k, x) if self.split else pl.ds(self.base + (turn + k) % 4 * self.blk, self.blk)

        def part(self, k, h):
            if self.split:
                start = self.base + x * (self.units // 2) + (turn + k) % 4 * self.hlf
                return pl.ds(start + h * (self.hlf // 2), self.hlf // 2)
            return self.half(k, h)

        def slab(self, j, where):
            return f_ref.at[(group + j) % 4, where]

        def same(self, key, ref, dp):
            self.send(key, ref, ref, dp)

        def rs(self):
            self.send("ra", d_ref.at[self.half(2, 0)], slot_a.at[self.eighth], right)
            self.send("rb", d_ref.at[self.half(2, 1)], slot_b.at[self.eighth], left)
            self.send("r1", d_ref.at[self.half(1, 1)], from_left.at[self.halves[1]], right)
            self.send("l0", d_ref.at[self.half(3, 0)], from_right.at[self.halves[0]], left)

        def rh1(self):
            self.arrive("ra")
            stage_r[self.eighth] = ring_add(d_ref[self.half(1, 0)], slot_a[self.eighth])
            self.send("r0", stage_r.at[self.eighth], from_left.at[self.halves[0]], right)

        def rh2(self):
            self.arrive("rb")
            stage_l[self.eighth] = ring_add(d_ref[self.half(3, 1)], slot_b[self.eighth])
            self.send("l1", stage_l.at[self.eighth], from_right.at[self.halves[1]], left)

        def other(self):
            return pl.ds(self.halves[0].start + (1 - x) * self.hlf, self.hlf)

        def own(self):
            return pl.ds(self.halves[0].start + x * self.hlf, self.hlf)

        def re(self):
            self.arrive("r1", "l0", "r0", "l1")
            for h, where in enumerate(self.halves):
                mine[0, where] = ring_add(d_ref[self.half(0, h)], from_left[where], from_right[where])
            if self.split:
                self.send("p", mine.at[0, self.other()], theirs.at[self.halves[0]], pair)
            else:
                self.send("p", mine.at[0, self.quarter], theirs.at[self.quarter], pair)

        def final(self):
            return mine.at[1, self.halves[0] if self.split else self.quarter]

        def keep(self):
            return pltpu.make_async_copy(self.final(), self.slab(0, self.block(0)), keep_sems.at[self.n])

        def gs(self):
            self.arrive("p")
            if self.split:
                mine[1, self.halves[0]] = ring_add(mine[0, self.own()], theirs[self.halves[0]])
            else:
                mine[1, self.quarter] = ring_add(mine[0, self.quarter], theirs[self.quarter])
            to = self.slab(0, self.block(0))
            self.send("gr", self.final(), to, right)
            self.send("gl", self.final(), to, left)
            self.send("u0", self.final(), to, up)
            self.send("d0", self.final(), to, down)
            self.keep().start()

        def h1(self):
            self.arrive("gr")
            self.same("hr", self.slab(0, self.part(3, 0)), right)

        def h2(self):
            self.arrive("gl")
            self.same("hl", self.slab(0, self.part(1, 1)), left)

        def s(self, k):
            self.arrive(*{1: ("gl",), 2: ("hr", "hl"), 3: ("gr",)}[k])
            self.same(f"u{k}", self.slab(0, self.block(k)), up)
            self.same(f"d{k}", self.slab(0, self.block(k)), down)

        def pu(self, k):
            self.arrive(f"u{k}")
            self.same(f"uu{k}", self.slab(3, self.part(k, 0)), up)

        def pd(self, k):
            self.arrive(f"d{k}")
            self.same(f"dd{k}", self.slab(1, self.part(k, 1)), down)

        def x(self, j):
            if j == 0:
                self.arrive("gr", "gl", "hr", "hl")
                self.keep().wait()
            elif j == 3:
                self.arrive("u0", "u1", "u2", "u3")
            elif j == 1:
                self.arrive("d0", "d1", "d2", "d3")
            else:
                self.arrive(*(f"{d}{k}" for d in ("uu", "dd") for k in range(4)))
            self.same(f"x{j}", self.slab(j, pl.ds(self.base + x * (self.units // 2), self.units // 2)), pair)

        def end(self):
            self.arrive(*self.copies)
            if not self.split:
                self.keep().wait()

    def small_copies(buf, peers, slot, base, src):
        buf[slot] = src[...]
        copies = []
        for k, dp in enumerate(peers):
            copies.append(remote(src, buf.at[slot], s_sends.at[base + k], s_recvs.at[base + k], dp, section, chan))
        for copy in copies:
            copy.start()
        return copies

    chunks = [Chunk(n) for n in range(len(CHUNKS))]

    weight_gradient(hidden_all, slice_lattice, d_ref, 2, 2, 1)
    weight_gradient(hidden_all, slice_lattice, d_ref, 2, 1, 1)
    chunks[0].rs()
    chunks[1].rs()
    weight_gradient(hidden_all, slice_lattice, d_ref, 2, 0, 1)
    weight_gradient(hidden_all, slice_lattice, d_ref, 1, 2, 1)
    weight_gradient(hidden_all, slice_lattice, d_ref, 1, 1, 2)
    chunks[2].rs()
    chunks[0].rh1()
    chunks[0].rh2()
    weight_gradient(hidden_all, slice_lattice, d_ref, 0, 2, 3)
    chunks[3].rs()
    chunks[1].rh1()
    chunks[1].rh2()
    chunks[4].rs()
    chunks[0].re()
    chunks[2].rh2()
    chunks[2].rh1()
    chunks[1].re()
    chunks[3].rh1()
    chunks[3].rh2()
    chunks[0].gs()
    @pl.when(section == 0)
    def _():
        for k in range(2):
            remote(adj_own, full.at[k], full_send.at[k], full_recv.at[k], here, 1, chan).wait_recv()
            fill(k, full[k].astype(F32))
        acc_g[...] = jnp.zeros_like(acc_g)

    chunks[4].rh1()
    chunks[4].rh2()
    chunks[2].re()
    chunks[1].gs()
    chunks[3].re()
    @pl.when(section == 0)
    def _():
        conv_transposed(lattice, weights, 0, acc_g, lambda t: None, (2,))

    chunks[0].h1()
    chunks[0].h2()
    chunks[0].s(3)
    chunks[0].s(1)
    chunks[0].pu(0)
    chunks[0].pd(0)
    @pl.when(section == 0)
    def _():
        conv_transposed(lattice, weights, 1, acc_g, lambda t: None, (2,))

    chunks[4].re()
    chunks[2].gs()
    chunks[1].h1()
    chunks[1].h2()
    chunks[1].s(3)
    @pl.when(section == 0)
    def _():
        conv_transposed(lattice, weights, 0, acc_g, lambda t: None, (1,))

    chunks[1].s(1)
    chunks[0].s(2)
    chunks[0].x(0)
    chunks[1].pu(0)
    chunks[1].pd(0)
    chunks[0].pu(3)
    chunks[0].pd(3)
    chunks[0].pu(1)
    chunks[0].pd(1)
    @pl.when(section == 0)
    def _():
        conv_transposed(lattice, weights, 1, acc_g, lambda t: None, (1,))

    chunks[3].gs()
    @pl.when(section == 0)
    def _():
        conv_transposed(lattice, weights, 0, acc_g, lambda t: None, (0,))

    chunks[1].s(2)
    chunks[2].h2()
    chunks[2].s(1)
    chunks[0].pu(2)
    chunks[0].pd(2)
    @pl.when(section == 0)
    def _():
        conv_transposed(lattice, weights, 1, acc_g, lambda t: None, (0,))

    chunks[0].x(3)
    chunks[0].x(1)
    chunks[2].h1()
    chunks[2].s(3)
    chunks[2].pu(0)
    chunks[2].pd(0)
    chunks[1].pd(3)
    chunks[1].pu(3)
    chunks[1].pu(1)
    chunks[1].pd(1)
    @pl.when(section == 0)
    def _():
        gain_sum, bias_sum = None, None
        for f in range(4):
            lanes = slice(128 * f, 128 * f + 128)
            normed = normed_s[:, :, lanes]
            unused, gain_term, bias_term = norm_backward(acc_g[:, lanes], normed, normed * gain + bias, gain)
            gain_sum = gain_term if gain_sum is None else gain_sum + gain_term
            bias_sum = bias_term if bias_sum is None else bias_sum + bias_term
        small_own[...] = small_rows(gain_sum, bias_sum)

    chunks[4].gs()
    chunks[0].x(2)
    first = small_copies(small_1, (right, opp, left), turn, 0, small_own)
    chunks[3].h1()
    chunks[3].s(3)
    chunks[1].pu(2)
    chunks[1].pd(2)
    chunks[2].s(2)
    chunks[2].x(0)
    chunks[3].h2()
    chunks[3].s(1)
    chunks[3].pu(0)
    chunks[3].pd(0)
    chunks[2].pu(1)
    chunks[2].pd(1)
    chunks[2].pu(3)
    chunks[2].pd(3)
    for copy in first:
        copy.wait()
    small_2[4] = small_1[0] + small_1[1] + small_1[2] + small_1[3]
    second = small_copies(small_2, (up, far, down), group, 3, small_2.at[4])
    chunks[2].pu(2)
    chunks[2].pd(2)
    chunks[2].x(3)
    chunks[2].x(1)
    chunks[3].s(2)
    chunks[4].h2()
    chunks[4].h1()
    chunks[4].s(3)
    chunks[4].s(1)
    chunks[3].pu(3)
    chunks[3].pd(3)
    chunks[3].pu(1)
    chunks[3].pd(1)
    chunks[4].pu(0)
    chunks[4].pd(0)
    chunks[2].x(2)
    chunks[3].pu(2)
    chunks[3].pd(2)
    for copy in second:
        copy.wait()
    small_3[0] = small_2[0] + small_2[1] + small_2[2] + small_2[3]
    third = remote(small_3.at[0], small_3.at[1], s_sends.at[6], s_recvs.at[6], pair, section, chan)
    third.start()
    chunks[4].s(2)
    chunks[4].pd(3)
    chunks[4].pu(3)
    chunks[4].pd(1)
    chunks[4].pu(1)
    chunks[4].pd(2)
    chunks[4].pu(2)
    for chunk in chunks:
        chunk.end()
    third.wait()
    small_out[...] = small_3[0] + small_3[1]

    @pl.when(section == 0)
    def _():
        for pair in range(2):
            for hh in range(2):
                conv_copy(hh, pair).wait_send()

    @pl.when(section == 1)
    def _():
        for jj in range(2):
            for k in range(2):

                @pl.when((2 * chan + jj != y) | (chan != k))
                def _(jj=jj, k=k):
                    cot_slice_copy(jj, k).wait_send()

                for pair in range(2):
                    adj_slice_copy(jj, k, pair).wait_send()
        for k in range(2):
            full_copy(k).wait_send()

    for pair in range(2):
        for step in (1, 2, 3):
            hidden_copy(step, pair).wait_send()
    for copy in started:
        copy.wait_send()


def step(clips, cot, gain, bias, weights):
    vmem = pl.BlockSpec(memory_space=pltpu.VMEM)
    dma = pltpu.SemaphoreType.DMA
    return pl.pallas_call(
        step_kernel,
        out_shape=(pltpu.VMEM((4, UNITS, 16, SLICE), BF), pltpu.VMEM((8, CH), F32)),
        in_specs=[vmem, vmem, vmem, vmem, pl.BlockSpec(memory_space=pl.ANY)],
        out_specs=(vmem, vmem),
        scratch_shapes=[
            pltpu.VMEM((27, CH, FULL), BF),
            pltpu.VMEM((2, 4, 10, 16, 3 * CH), BF),
            pltpu.VMEM((4, 4, 10, 16, 3 * SLICE), BF),
            pltpu.VMEM((CH, POS), BF),
            pltpu.VMEM((CH, 4 * POS), BF),
            pltpu.VMEM((POS, CH), BF),
            pltpu.VMEM((2, POS, CH), BF),
            pltpu.VMEM((4, POS, SLICE), BF),
            pltpu.VMEM((2, POS, CH), BF),
            pltpu.VMEM((2, POS, CH), BF),
            pltpu.VMEM((POS, CH), F32),
            pltpu.VMEM((CH, POS), F32),
            pltpu.VMEM((GROUP, GROUP, POS), F32),
            pltpu.VMEM((4 * CH, 128), F32),
            pltpu.VMEM((4 * CH, 128), F32),
            pltpu.VMEM((POS, CH), BF),
            pltpu.VMEM((8, CH), F32),
            pltpu.VMEM((4, 8, CH), F32),
            pltpu.VMEM((5, 8, CH), F32),
            pltpu.VMEM((2, 8, CH), F32),
            pltpu.VMEM((UNITS, 16, SLICE), BF),
            pltpu.VMEM((UNITS // 8, 16, SLICE), BF),
            pltpu.VMEM((UNITS // 8, 16, SLICE), BF),
            pltpu.VMEM((UNITS // 4, 16, SLICE), BF),
            pltpu.VMEM((UNITS // 4, 16, SLICE), BF),
            pltpu.VMEM((UNITS // 8, 16, SLICE), BF),
            pltpu.VMEM((UNITS // 8, 16, SLICE), BF),
            pltpu.VMEM((2, UNITS // 4, 16, SLICE), BF),
            pltpu.VMEM((UNITS // 4, 16, SLICE), BF),
            dma((3,)), dma((2,)), dma((2,)), dma((2,)), dma((4,)), dma((4,)), dma((2, 4)), dma((2, 4)), dma((2, 3)), dma((2, 4)),
            dma((2, 2)), dma((2, 2)),
            dma((len(CHUNKS), 32)), dma((len(CHUNKS), 32)), dma((len(CHUNKS),)), dma((7,)), dma((7,)),
        ],
        compiler_params=pltpu.CompilerParams(collective_id=1, has_side_effects=True, vmem_limit_bytes=48 << 20),
        name="step",
    )(clips, cot, gain, bias, weights)


def widen_kernel(slabs, sums, out, gain_out, bias_out, buffers, sems):
    units = UNITS // WIDEN
    rows = units * 16
    gain_out[...] = sums[0:1]
    bias_out[...] = sums[1:2]

    def copy(i):
        return pltpu.make_async_copy(buffers.at[i % SLOTS], out.at[pl.ds(i * rows, rows)], sems.at[i % SLOTS])

    for i in range(WIDEN):
        if i >= SLOTS:
            copy(i - SLOTS).wait()
        for k in range(4):
            block = slabs[k, i * units : (i + 1) * units].reshape(rows, SLICE)
            buffers[i % SLOTS, :, k * SLICE : (k + 1) * SLICE] = block.astype(F32)
        copy(i).start()
    for i in range(WIDEN - SLOTS, WIDEN):
        copy(i).wait()


def widen(slabs, sums):
    vmem = pl.BlockSpec(memory_space=pltpu.VMEM)
    rows = UNITS // WIDEN * 16
    return pl.pallas_call(
        widen_kernel,
        out_shape=(
            jax.ShapeDtypeStruct((UNITS * 16, FULL), F32),
            jax.ShapeDtypeStruct((1, CH), F32),
            jax.ShapeDtypeStruct((1, CH), F32),
        ),
        in_specs=[vmem, vmem],
        out_specs=(pl.BlockSpec(memory_space=pl.ANY), vmem, vmem),
        scratch_shapes=[pltpu.VMEM((SLOTS, rows, FULL), F32), pltpu.SemaphoreType.DMA((SLOTS,))],
        compiler_params=pltpu.CompilerParams(vmem_limit_bytes=20 << 20),
        name="widen",
    )(slabs, sums)


def shards(clips, conv_weight, norm_gain, norm_bias, cotangent):
    slabs, sums = step(clips.reshape(4 * CH, 128), cotangent.reshape(4 * CH, 128), norm_gain, norm_bias, conv_weight[0])
    weight_grad, gain_grad, bias_grad = widen(slabs, sums)
    return weight_grad.reshape(1, 27, CH, FULL), gain_grad, bias_grad


def solution(mesh):
    in_specs = (
        P("dp", "chan", None, None),
        P("section", None, "chan", None),
        P("section", "chan"),
        P("section", "chan"),
        P("dp", "chan", None, None),
    )
    out_specs = (P("section", None, "chan", None), P("section", "chan"), P("section", "chan"))
    return jax.shard_map(shards, mesh=mesh, in_specs=in_specs, out_specs=out_specs, check_vma=False)
```

```python
import jax
import jax.numpy as jnp
from jax import lax
from jax.experimental import pallas as pl
from jax.experimental.pallas import tpu as pltpu
from jax.sharding import PartitionSpec as P

EPSILON = 1e-05
MESH = pl.DeviceIdType.MESH
BF = jnp.bfloat16
F32 = jnp.float32

CH = 256
FULL = 512
POS = 512
SLICE = 128
GROUP = 16
UNITS = 432
CHUNKS = ((48, True), (48, False), (96, True), (96, False), (144, False))
WIDEN = 27
SLOTS = 6


def coords():
    dp = lax.axis_index("dp")
    return dp // 8, dp // 2 % 4, dp % 2, lax.axis_index("section"), lax.axis_index("chan")


def remote(src, dst, send_sem, recv_sem, dp, section, chan):
    return pltpu.make_async_remote_copy(
        src_ref=src,
        dst_ref=dst,
        send_sem=send_sem,
        recv_sem=recv_sem,
        device_id={"dp": dp, "section": section, "chan": chan},
        device_id_type=MESH,
    )


def norm_frame(values):
    scale = 1.0 / (GROUP * 128)
    centre = jnp.sum(values, axis=(1, 2), keepdims=True) * scale
    moved = values - centre
    spread = jnp.sum(moved * moved, axis=(1, 2), keepdims=True) * scale
    inv_std = lax.rsqrt(spread + EPSILON)
    return moved * inv_std, inv_std


def silu(shifted):
    return shifted * (1.0 / (1.0 + jnp.exp(-shifted)))


def norm_forward(act, gain, bias):
    normed, inv_std = norm_frame(act.reshape(GROUP, GROUP, 128))
    return normed, normed * gain + bias, inv_std


def norm_backward(grad_hidden, normed, shifted, gain):
    sig = 1.0 / (1.0 + jnp.exp(-shifted))
    grad_shift = grad_hidden.reshape(GROUP, GROUP, 128) * sig * (1.0 + shifted * (1.0 - sig))
    gain_term = jnp.sum(grad_shift * normed, axis=2, keepdims=True)
    bias_term = jnp.sum(grad_shift, axis=2, keepdims=True)
    return grad_shift * gain, gain_term, bias_term


def norm_input_grad(grad_normed, normed, inv_std):
    scale = 1.0 / (GROUP * 128)
    mean_grad = jnp.sum(grad_normed, axis=(1, 2), keepdims=True) * scale
    mean_cross = jnp.sum(grad_normed * normed, axis=(1, 2), keepdims=True) * scale
    return (grad_normed - mean_grad - normed * mean_cross) * inv_std


def small_rows(gain_term, bias_term):
    lane = lax.broadcasted_iota(jnp.int32, (CH, 128), 1)
    gain_col = jnp.broadcast_to(gain_term.reshape(CH, 1), (CH, 128))
    bias_col = jnp.broadcast_to(bias_term.reshape(CH, 1), (CH, 128))
    both = jnp.where(lane == 0, gain_col, jnp.where(lane == 1, bias_col, 0.0))
    return both.T[:8]


def shifted_columns(values, store):
    col = lax.broadcasted_iota(jnp.int32, values.shape, 0) % 16
    store(0, jnp.where(col == 0, 0.0, pltpu.roll(values, 1, 0)))
    store(1, values)
    store(2, jnp.where(col == 15, 0.0, pltpu.roll(values, POS - 1, 0)))


def column(row):
    return jnp.broadcast_to(row, (128, CH)).T.reshape(GROUP, GROUP, 128)


def conv_forward(lattice, weights, start, pair, acc, wait_weights):
    for t in (2, 1, 0)[: 2 + pair]:
        wait_weights(t)
        frame_in = max(2 * pair + t - 2, 0)
        frame_out = frame_in + 2 - t
        count = 2 * pair + 2 - frame_out
        rows = 128 * count

        def tap_row(r, carry, t=t, frame_in=frame_in, frame_out=frame_out, count=count, rows=rows):
            lhs = lattice[0, frame_in : frame_in + count, pl.ds(r, 8)].reshape(rows, 3 * CH)
            rhs = weights[pl.ds(9 * t + 3 * r, 3), :, pl.ds(start, CH)].reshape(3 * CH, CH)
            part = jnp.dot(lhs, rhs, preferred_element_type=F32)
            acc[pl.ds(128 * frame_out, rows)] = acc[pl.ds(128 * frame_out, rows)] + part
            return carry

        lax.fori_loop(0, 3, tap_row, 0)


def conv_transposed(lattice, weights, half, acc, wait_weights, steps=(2, 1, 0)):
    start = pl.multiple_of(half * CH, CH)
    for t in steps:
        wait_weights(t)
        cols = 128 * (t + 2)

        def tap_row(r, carry, t=t, cols=cols):
            part = None
            for v in range(3):
                rhs = lattice[half, 2 - t : 4, pl.ds(2 - r, 8), :, v * CH : (v + 1) * CH].reshape(cols, CH)
                one = lax.dot_general(
                    weights[9 * t + 3 * r + 2 - v, :, pl.ds(start, CH)], rhs, (((1,), (1,)), ((), ())),
                    preferred_element_type=F32,
                )
                part = one if part is None else part + one
            acc[:, 0:cols] = acc[:, 0:cols] + part
            return carry

        lax.fori_loop(0, 3, tap_row, 0)


def weight_gradient(hidden_all, lattice, out, t, first, count):
    cols = 128 * (t + 2)
    lhs = jnp.concatenate([hidden_all[:, POS * k : POS * k + cols] for k in range(4)], axis=1)

    def tap_row(step, carry):
        r = first + step
        rhs = lattice[:, 2 - t : 4, pl.ds(2 - r, 8)].reshape(4 * cols, 3 * SLICE)
        part = jnp.dot(lhs, rhs, preferred_element_type=F32).astype(BF)
        for v in range(3):
            tap = 9 * t + 3 * r + 2 - v
            out[pl.ds(16 * tap, 16)] = part[:, v * SLICE : (v + 1) * SLICE].reshape(16, 16, SLICE)
        return carry

    if count == 1:
        tap_row(0, 0)
    else:
        lax.fori_loop(0, count, tap_row, 0)


def ring_add(*terms):
    total = terms[0].astype(F32)
    for term in terms[1:]:
        total = total + term.astype(F32)
    return total.astype(BF)


def step_kernel(
    clips_ref, cot_ref, gain_ref, bias_ref, w_hbm, f_ref, small_out,
    weights, lattice, slice_lattice, hidden_own, hidden_all, adj_own, full, slices, conv_out, conv_in, acc_y, acc_g, normed_s, raw, raw_cot, adj_new,
    small_own, small_1, small_2, small_3, d_ref, slot_a, slot_b, from_left, from_right, stage_r, stage_l, mine, theirs,
    w_sems, own_sems, full_send, full_recv, slice_send, slice_recv, adj_send, adj_recv, hid_send, hid_recv, y_send, y_recv,
    sends, recvs, keep_sems, s_sends, s_recvs,
):
    z, y, x, section, chan = coords()
    here = z * 8 + y * 2 + x

    def at_z(k):
        return k * 8 + y * 2 + x

    def at_y(k):
        return z * 8 + k * 2 + x

    barrier = pltpu.get_barrier_semaphore()

    def w_copy(t):
        return pltpu.make_async_copy(w_hbm.at[pl.ds(9 * t, 9)], weights.at[pl.ds(9 * t, 9)], w_sems.at[t])

    for t in (2, 1, 0):
        w_copy(t).start()

    def greet(dp, s, c):
        pl.semaphore_signal(barrier, inc=1, device_id={"dp": dp, "section": s, "chan": c}, device_id_type=MESH)

    for s in (0, 1):
        for c in (0, 1):
            for step in (1, 2, 3):
                greet(at_z((z + step) % 4), s, c)
                greet(at_y((y + step) % 4), s, c)
    greet(here, 1 - section, chan)
    greet(here, section, 1 - chan)
    greet(here, 1 - section, 1 - chan)
    greet(z * 8 + y * 2 + 1 - x, section, chan)

    def wait_weights(t):
        w_copy(t).wait()

    gain = column(gain_ref[...])
    bias = column(bias_ref[...])

    group = section * y + (1 - section) * z

    def ring(k):
        return section * at_y(k) + (1 - section) * at_z(k)

    def frames(pair, at):
        return pl.ds(pl.multiple_of(at * POS + 256 * pair, 256), 256)

    def hidden_copy(step, pair):
        return remote(
            hidden_own.at[:, pl.ds(256 * pair, 256)], hidden_all.at[:, frames(pair, group)],
            hid_send.at[pair, step - 1], hid_recv.at[pair, (4 - step) % 4], ring((group + step) % 4), section, chan,
        )

    def hidden_arrival(step, pair):
        return remote(
            hidden_own.at[:, pl.ds(256 * pair, 256)], hidden_all.at[:, frames(pair, (group + step) % 4)],
            hid_send.at[pair, step - 1], hid_recv.at[pair, step], ring((group + step) % 4), section, chan,
        )

    def hidden_own_copy(pair):
        return pltpu.make_async_copy(
            hidden_own.at[:, pl.ds(256 * pair, 256)], hidden_all.at[:, frames(pair, group)], own_sems.at[pair]
        )

    def full_copy(c):
        return remote(adj_new, full.at[chan], full_send.at[c], full_recv.at[chan], here, 0, c)

    def cot_full_copy():
        return remote(adj_own, full.at[chan], full_send.at[0], full_recv.at[chan], here, 1, 1 - chan)

    def cot_slice_copy(jj, c):
        return remote(
            adj_own.at[:, pl.ds(SLICE * jj, SLICE)], slices.at[y], slice_send.at[2 * jj + c], slice_recv.at[y],
            at_y(2 * chan + jj), 1, c,
        )

    def adj_slice_copy(jj, c, pair):
        rows = pl.ds(256 * pair, 256)
        return remote(
            adj_new.at[rows, pl.ds(SLICE * jj, SLICE)], slices.at[z, rows], adj_send.at[pair, 2 * jj + c],
            adj_recv.at[pair, z], at_z(2 * chan + jj), 0, c,
        )

    def own_slice_copy():
        return pltpu.make_async_copy(
            adj_own.at[:, pl.ds(pl.multiple_of(y % 2 * SLICE, SLICE), SLICE)], slices.at[y], own_sems.at[2]
        )

    def conv_half(hh):
        return hh * chan + (1 - hh) * (1 - chan)

    def conv_copy(hh, pair):
        rows = pl.ds(256 * pair, 256)
        return remote(
            conv_out.at[hh, rows], conv_in.at[chan, rows], y_send.at[pair, hh], y_recv.at[pair, chan], here, 1, conv_half(hh)
        )

    def conv_arrival(c, pair):
        rows = pl.ds(256 * pair, 256)
        return remote(conv_out.at[c, rows], conv_in.at[c, rows], y_send.at[pair, c], y_recv.at[pair, c], here, 1, c)

    def frame(buffer, f):
        return buffer[pl.ds(f, CH, stride=4), :]

    zero_row = jnp.zeros((2, 4, 1, 16, 3 * CH), BF)
    lattice[:, :, 0:1] = zero_row
    lattice[:, :, 9:10] = zero_row
    zero_slice = jnp.zeros((4, 4, 1, 16, 3 * SLICE), BF)
    slice_lattice[:, :, 0:1] = zero_slice
    slice_lattice[:, :, 9:10] = zero_slice

    def fill(half, values):
        def store(v, moved):
            lattice[half, :, 1:9, :, v * CH : (v + 1) * CH] = moved.astype(BF).reshape(4, 8, 16, CH)

        shifted_columns(values, store)

    raw[...] = clips_ref[...].astype(F32)

    @pl.when(section == 0)
    def _():
        for f in range(4):
            lanes = slice(128 * f, 128 * f + 128)
            normed, shifted, inv_std = norm_forward(frame(raw, f), gain, bias)
            hidden_own[:, lanes] = silu(shifted).astype(BF).reshape(CH, 128)
            normed_s[:, :, lanes] = normed

    @pl.when(section == 1)
    def _():
        raw_cot[...] = cot_ref[...].astype(F32)
        for f in range(4):
            adj_own[128 * f : 128 * f + 128] = frame(raw_cot, f).T.astype(BF)

    pl.semaphore_wait(barrier, 28)

    @pl.when(section == 0)
    def _():
        for pair in range(2):
            for step in (1, 2, 3):
                hidden_copy(step, pair).start()
            hidden_own_copy(pair).start()
        fill(0, hidden_own[...].astype(F32).T)
        for pair in range(2):
            for hh in range(2):
                rows = slice(256 * pair, 256 * pair + 256)
                acc_y[rows] = jnp.zeros((256, CH), F32)
                start = pl.multiple_of(conv_half(hh) * CH, CH)

                def first_use(t, pair=pair, hh=hh):
                    if hh == 0 and (t == 0) == (pair == 1):
                        wait_weights(t)

                conv_forward(lattice, weights, start, pair, acc_y, first_use)
                conv_out[hh, rows] = acc_y[rows].astype(BF)
                conv_copy(hh, pair).start()

    @pl.when(section == 1)
    def _():
        cot_full_copy().start()
        for jj in range(2):
            for c in range(2):

                @pl.when((2 * chan + jj != y) | (chan != c))
                def _(jj=jj, c=c):
                    cot_slice_copy(jj, c).start()

        @pl.when(y // 2 == chan)
        def _():
            own_slice_copy().start()

        fill(chan, adj_own[...].astype(F32))
        acc_g[...] = jnp.zeros_like(acc_g)
        conv_transposed(lattice, weights, chan, acc_g, wait_weights)
        remote(adj_own, full.at[1 - chan], full_send.at[0], full_recv.at[1 - chan], here, 1, 1 - chan).wait_recv()
        fill(1 - chan, full[1 - chan].astype(F32))
        conv_transposed(lattice, weights, 1 - chan, acc_g, lambda t: None)
        gain_sum, bias_sum = None, None
        for pair in range(2):
            for c in range(2):
                conv_arrival(c, pair).wait_recv()
            saved = []
            for f in (2 * pair, 2 * pair + 1):
                rows = slice(128 * f, 128 * f + 128)
                summed = conv_in[0, rows].astype(F32) + conv_in[1, rows].astype(F32)
                act = (frame(raw, f) + summed.T).astype(BF).astype(F32)
                parts = norm_forward(act, gain, bias)
                hidden_own[:, rows] = silu(parts[1]).astype(BF).reshape(CH, 128)
                saved.append((f, rows, parts))
            for step in (1, 2, 3):
                hidden_copy(step, pair).start()
            hidden_own_copy(pair).start()
            for f, rows, (normed, shifted, inv_std) in saved:
                grad_normed, gain_term, bias_term = norm_backward(acc_g[:, rows], normed, shifted, gain)
                grad_act = norm_input_grad(grad_normed, normed, inv_std).reshape(CH, 128)
                adj_new[rows] = (frame(raw_cot, f) + grad_act).T.astype(BF)
                gain_sum = gain_term if gain_sum is None else gain_sum + gain_term
                bias_sum = bias_term if bias_sum is None else bias_sum + bias_term
            for jj in range(2):
                for c in range(2):
                    adj_slice_copy(jj, c, pair).start()
        for c in range(2):
            if c == 0:
                cot_full_copy().wait_send()
            full_copy(c).start()
        small_own[...] = small_rows(gain_sum, bias_sum)
        for k in range(4):

            @pl.when((k != y) | (y // 2 != chan))
            def _(k=k):
                remote(
                    adj_own.at[:, pl.ds(0, SLICE)], slices.at[k], slice_send.at[0], slice_recv.at[k], here, 1, 1 - chan
                ).wait_recv()

        @pl.when(y // 2 == chan)
        def _():
            own_slice_copy().wait()

    @pl.when(section == 0)
    def _():
        for k in range(4):
            for pair in range(2):
                rows = pl.ds(256 * pair, 256)
                remote(
                    adj_new.at[rows, pl.ds(0, SLICE)], slices.at[k, rows], adj_send.at[pair, 0], adj_recv.at[pair, k],
                    here, 1, chan,
                ).wait_recv()

    for k in range(4):

        def store(v, moved, k=k):
            slice_lattice[k, :, 1:9, :, v * SLICE : (v + 1) * SLICE] = moved.astype(BF).reshape(4, 8, 16, SLICE)

        shifted_columns(slices[k].astype(F32), store)
    def hidden_here(pair):
        hidden_own_copy(pair).wait()
        for step in (1, 2, 3):
            hidden_arrival(step, pair).wait_recv()

    hidden_here(0)

    turn = section * z + (1 - section) * y

    def along(step):
        return section * at_z((z + step) % 4) + (1 - section) * at_y((y + step) % 4)

    def across(step):
        return section * at_y((y + step) % 4) + (1 - section) * at_z((z + step) % 4)

    right, left, opp = along(1), along(3), along(2)
    up, down, far = across(1), across(3), across(2)
    pair = z * 8 + y * 2 + 1 - x
    started = []

    class Chunk:
        def __init__(self, n):
            before = sum(c[0] for c in CHUNKS[:n])
            self.n, self.copies, self.here = n, {}, set()
            self.units, self.split = CHUNKS[n]
            self.base = before
            self.blk, self.hlf = self.units // 4, self.units // 8
            self.eighth = pl.ds(before // 8, self.hlf)
            self.quarter = pl.ds(before // 4, self.blk)
            self.halves = (pl.ds(before // 4, self.hlf), pl.ds(before // 4 + self.hlf, self.hlf))

        def send(self, key, src, dst, dp):
            k = len(self.copies)
            copy = remote(src, dst, sends.at[self.n, k], recvs.at[self.n, k], dp, section, chan)
            copy.start()
            self.copies[key] = copy
            started.append(copy)
            if len(started) > 30:
                started[len(started) - 31].wait_send()

        def arrive(self, *keys):
            for key in keys:
                if key not in self.here:
                    self.here.add(key)
                    self.copies[key].wait_recv()

        def half(self, k, h):
            place = (turn + k) % 4
            if self.split:
                return pl.ds(self.base + h * (self.units // 2) + place * self.hlf, self.hlf)
            return pl.ds(self.base + place * self.blk + h * self.hlf, self.hlf)

        def block(self, k):
            return self.half(k, x) if self.split else pl.ds(self.base + (turn + k) % 4 * self.blk, self.blk)

        def part(self, k, h):
            if self.split:
                start = self.base + x * (self.units // 2) + (turn + k) % 4 * self.hlf
                return pl.ds(start + h * (self.hlf // 2), self.hlf // 2)
            return self.half(k, h)

        def slab(self, j, where):
            return f_ref.at[(group + j) % 4, where]

        def same(self, key, ref, dp):
            self.send(key, ref, ref, dp)

        def rs(self):
            self.send("ra", d_ref.at[self.half(2, 0)], slot_a.at[self.eighth], right)
            self.send("rb", d_ref.at[self.half(2, 1)], slot_b.at[self.eighth], left)
            self.send("r1", d_ref.at[self.half(1, 1)], from_left.at[self.halves[1]], right)
            self.send("l0", d_ref.at[self.half(3, 0)], from_right.at[self.halves[0]], left)

        def rh1(self):
            self.arrive("ra")
            stage_r[self.eighth] = ring_add(d_ref[self.half(1, 0)], slot_a[self.eighth])
            self.send("r0", stage_r.at[self.eighth], from_left.at[self.halves[0]], right)

        def rh2(self):
            self.arrive("rb")
            stage_l[self.eighth] = ring_add(d_ref[self.half(3, 1)], slot_b[self.eighth])
            self.send("l1", stage_l.at[self.eighth], from_right.at[self.halves[1]], left)

        def other(self):
            return pl.ds(self.halves[0].start + (1 - x) * self.hlf, self.hlf)

        def own(self):
            return pl.ds(self.halves[0].start + x * self.hlf, self.hlf)

        def re(self):
            self.arrive("r1", "l0", "r0", "l1")
            for h, where in enumerate(self.halves):
                mine[0, where] = ring_add(d_ref[self.half(0, h)], from_left[where], from_right[where])
            if self.split:
                self.send("p", mine.at[0, self.other()], theirs.at[self.halves[0]], pair)
            else:
                self.send("p", mine.at[0, self.quarter], theirs.at[self.quarter], pair)

        def final(self):
            return mine.at[1, self.halves[0] if self.split else self.quarter]

        def keep(self):
            return pltpu.make_async_copy(self.final(), self.slab(0, self.block(0)), keep_sems.at[self.n])

        def gs(self):
            self.arrive("p")
            if self.split:
                mine[1, self.halves[0]] = ring_add(mine[0, self.own()], theirs[self.halves[0]])
            else:
                mine[1, self.quarter] = ring_add(mine[0, self.quarter], theirs[self.quarter])
            to = self.slab(0, self.block(0))
            self.send("gr", self.final(), to, right)
            self.send("gl", self.final(), to, left)
            self.send("u0", self.final(), to, up)
            self.send("d0", self.final(), to, down)
            self.keep().start()

        def h1(self):
            self.arrive("gr")
            self.same("hr", self.slab(0, self.part(3, 0)), right)

        def h2(self):
            self.arrive("gl")
            self.same("hl", self.slab(0, self.part(1, 1)), left)

        def s(self, k):
            self.arrive(*{1: ("gl",), 2: ("hr", "hl"), 3: ("gr",)}[k])
            self.same(f"u{k}", self.slab(0, self.block(k)), up)
            self.same(f"d{k}", self.slab(0, self.block(k)), down)

        def pu(self, k):
            self.arrive(f"u{k}")
            self.same(f"uu{k}", self.slab(3, self.part(k, 0)), up)

        def pd(self, k):
            self.arrive(f"d{k}")
            self.same(f"dd{k}", self.slab(1, self.part(k, 1)), down)

        def x(self, j):
            if j == 0:
                self.arrive("gr", "gl", "hr", "hl")
                self.keep().wait()
            elif j == 3:
                self.arrive("u0", "u1", "u2", "u3")
            elif j == 1:
                self.arrive("d0", "d1", "d2", "d3")
            else:
                self.arrive(*(f"{d}{k}" for d in ("uu", "dd") for k in range(4)))
            self.same(f"x{j}", self.slab(j, pl.ds(self.base + x * (self.units // 2), self.units // 2)), pair)

        def end(self):
            self.arrive(*self.copies)
            if not self.split:
                self.keep().wait()

    def small_copies(buf, peers, slot, base, src):
        buf[slot] = src[...]
        copies = []
        for k, dp in enumerate(peers):
            copies.append(remote(src, buf.at[slot], s_sends.at[base + k], s_recvs.at[base + k], dp, section, chan))
        for copy in copies:
            copy.start()
        return copies

    chunks = [Chunk(n) for n in range(len(CHUNKS))]

    weight_gradient(hidden_all, slice_lattice, d_ref, 0, 0, 1)
    chunks[0].rs()
    weight_gradient(hidden_all, slice_lattice, d_ref, 0, 1, 1)
    chunks[1].rs()
    weight_gradient(hidden_all, slice_lattice, d_ref, 0, 2, 1)
    hidden_here(1)
    weight_gradient(hidden_all, slice_lattice, d_ref, 1, 0, 1)
    chunks[2].rs()
    weight_gradient(hidden_all, slice_lattice, d_ref, 1, 1, 1)
    weight_gradient(hidden_all, slice_lattice, d_ref, 1, 2, 1)
    chunks[3].rs()
    weight_gradient(hidden_all, slice_lattice, d_ref, 2, 0, 1)
    chunks[0].rh1()
    chunks[0].rh2()
    chunks[1].rh1()
    chunks[1].rh2()
    weight_gradient(hidden_all, slice_lattice, d_ref, 2, 1, 1)
    weight_gradient(hidden_all, slice_lattice, d_ref, 2, 2, 1)
    chunks[2].rh1()
    chunks[2].rh2()
    chunks[4].rs()
    chunks[0].re()
    chunks[1].re()
    chunks[3].rh1()
    chunks[3].rh2()
    chunks[2].re()
    chunks[0].gs()
    chunks[4].rh1()
    chunks[4].rh2()
    chunks[3].re()
    chunks[1].gs()
    chunks[2].gs()
    chunks[0].h2()
    chunks[0].h1()
    chunks[0].s(3)
    chunks[0].s(1)
    chunks[0].pu(0)
    chunks[0].pd(0)
    chunks[4].re()
    chunks[1].h1()
    chunks[1].h2()
    chunks[1].s(3)
    chunks[1].s(1)
    chunks[1].pu(0)
    chunks[1].pd(0)
    chunks[3].gs()
    chunks[0].s(2)
    chunks[0].x(0)
    chunks[0].pu(3)
    chunks[0].pd(3)
    chunks[0].pu(1)
    @pl.when(section == 0)
    def _():
        for k in range(2):
            remote(adj_own, full.at[k], full_send.at[k], full_recv.at[k], here, 1, chan).wait_recv()
            fill(k, full[k].astype(F32))
        acc_g[...] = jnp.zeros_like(acc_g)

    chunks[0].pd(1)
    chunks[2].h1()
    chunks[2].h2()
    chunks[2].s(3)
    chunks[2].s(1)
    chunks[2].pu(0)
    chunks[2].pd(0)
    chunks[1].s(2)
    @pl.when(section == 0)
    def _():
        conv_transposed(lattice, weights, 0, acc_g, lambda t: None, (2,))

    @pl.when(section == 0)
    def _():
        conv_transposed(lattice, weights, 1, acc_g, lambda t: None, (2,))

    chunks[0].pu(2)
    chunks[0].pd(2)
    chunks[0].x(3)
    chunks[0].x(1)
    chunks[1].pu(3)
    chunks[1].pd(3)
    @pl.when(section == 0)
    def _():
        conv_transposed(lattice, weights, 0, acc_g, lambda t: None, (1,))

    chunks[1].pu(1)
    chunks[1].pd(1)
    chunks[2].s(2)
    chunks[2].x(0)
    chunks[4].gs()
    @pl.when(section == 0)
    def _():
        conv_transposed(lattice, weights, 1, acc_g, lambda t: None, (1,))

    chunks[2].pu(3)
    chunks[2].pd(3)
    chunks[0].x(2)
    chunks[2].pu(1)
    chunks[2].pd(1)
    chunks[1].pu(2)
    chunks[1].pd(2)
    @pl.when(section == 0)
    def _():
        conv_transposed(lattice, weights, 0, acc_g, lambda t: None, (0,))

    chunks[3].h1()
    chunks[3].s(3)
    chunks[3].h2()
    chunks[3].s(1)
    chunks[3].pu(0)
    chunks[3].pd(0)
    @pl.when(section == 0)
    def _():
        conv_transposed(lattice, weights, 1, acc_g, lambda t: None, (0,))

    chunks[2].pu(2)
    chunks[2].pd(2)
    chunks[2].x(3)
    chunks[2].x(1)
    @pl.when(section == 0)
    def _():
        gain_sum, bias_sum = None, None
        for f in range(4):
            lanes = slice(128 * f, 128 * f + 128)
            normed = normed_s[:, :, lanes]
            unused, gain_term, bias_term = norm_backward(acc_g[:, lanes], normed, normed * gain + bias, gain)
            gain_sum = gain_term if gain_sum is None else gain_sum + gain_term
            bias_sum = bias_term if bias_sum is None else bias_sum + bias_term
        small_own[...] = small_rows(gain_sum, bias_sum)

    first = small_copies(small_1, (right, opp, left), turn, 0, small_own)
    chunks[3].s(2)
    chunks[2].x(2)
    chunks[3].pu(3)
    chunks[3].pd(3)
    for copy in first:
        copy.wait()
    small_2[4] = small_1[0] + small_1[1] + small_1[2] + small_1[3]
    second = small_copies(small_2, (up, far, down), group, 3, small_2.at[4])
    chunks[3].pu(1)
    chunks[3].pd(1)
    chunks[4].h1()
    chunks[4].h2()
    chunks[4].s(3)
    chunks[4].s(1)
    chunks[4].pu(0)
    chunks[4].pd(0)
    chunks[3].pu(2)
    chunks[3].pd(2)
    for copy in second:
        copy.wait()
    small_3[0] = small_2[0] + small_2[1] + small_2[2] + small_2[3]
    third = remote(small_3.at[0], small_3.at[1], s_sends.at[6], s_recvs.at[6], pair, section, chan)
    third.start()
    chunks[4].s(2)
    chunks[4].pu(3)
    chunks[4].pu(1)
    chunks[4].pd(3)
    chunks[4].pd(1)
    chunks[4].pu(2)
    chunks[4].pd(2)
    for chunk in chunks:
        chunk.end()
    third.wait()
    small_out[...] = small_3[0] + small_3[1]

    @pl.when(section == 0)
    def _():
        for pair in range(2):
            for hh in range(2):
                conv_copy(hh, pair).wait_send()

    @pl.when(section == 1)
    def _():
        for jj in range(2):
            for k in range(2):

                @pl.when((2 * chan + jj != y) | (chan != k))
                def _(jj=jj, k=k):
                    cot_slice_copy(jj, k).wait_send()

                for pair in range(2):
                    adj_slice_copy(jj, k, pair).wait_send()
        for k in range(2):
            full_copy(k).wait_send()

    for pair in range(2):
        for step in (1, 2, 3):
            hidden_copy(step, pair).wait_send()
    for copy in started[-30:]:
        copy.wait_send()


def step(clips, cot, gain, bias, weights):
    vmem = pl.BlockSpec(memory_space=pltpu.VMEM)
    dma = pltpu.SemaphoreType.DMA
    return pl.pallas_call(
        step_kernel,
        out_shape=(pltpu.VMEM((4, UNITS, 16, SLICE), BF), pltpu.VMEM((8, CH), F32)),
        in_specs=[vmem, vmem, vmem, vmem, pl.BlockSpec(memory_space=pl.ANY)],
        out_specs=(vmem, vmem),
        scratch_shapes=[
            pltpu.VMEM((27, CH, FULL), BF),
            pltpu.VMEM((2, 4, 10, 16, 3 * CH), BF),
            pltpu.VMEM((4, 4, 10, 16, 3 * SLICE), BF),
            pltpu.VMEM((CH, POS), BF),
            pltpu.VMEM((CH, 4 * POS), BF),
            pltpu.VMEM((POS, CH), BF),
            pltpu.VMEM((2, POS, CH), BF),
            pltpu.VMEM((4, POS, SLICE), BF),
            pltpu.VMEM((2, POS, CH), BF),
            pltpu.VMEM((2, POS, CH), BF),
            pltpu.VMEM((POS, CH), F32),
            pltpu.VMEM((CH, POS), F32),
            pltpu.VMEM((GROUP, GROUP, POS), F32),
            pltpu.VMEM((4 * CH, 128), F32),
            pltpu.VMEM((4 * CH, 128), F32),
            pltpu.VMEM((POS, CH), BF),
            pltpu.VMEM((8, CH), F32),
            pltpu.VMEM((4, 8, CH), F32),
            pltpu.VMEM((5, 8, CH), F32),
            pltpu.VMEM((2, 8, CH), F32),
            pltpu.VMEM((UNITS, 16, SLICE), BF),
            pltpu.VMEM((UNITS // 8, 16, SLICE), BF),
            pltpu.VMEM((UNITS // 8, 16, SLICE), BF),
            pltpu.VMEM((UNITS // 4, 16, SLICE), BF),
            pltpu.VMEM((UNITS // 4, 16, SLICE), BF),
            pltpu.VMEM((UNITS // 8, 16, SLICE), BF),
            pltpu.VMEM((UNITS // 8, 16, SLICE), BF),
            pltpu.VMEM((2, UNITS // 4, 16, SLICE), BF),
            pltpu.VMEM((UNITS // 4, 16, SLICE), BF),
            dma((3,)), dma((3,)), dma((2,)), dma((2,)), dma((4,)), dma((4,)), dma((2, 4)), dma((2, 4)), dma((2, 3)), dma((2, 4)),
            dma((2, 2)), dma((2, 2)),
            dma((len(CHUNKS), 32)), dma((len(CHUNKS), 32)), dma((len(CHUNKS),)), dma((7,)), dma((7,)),
        ],
        compiler_params=pltpu.CompilerParams(collective_id=1, has_side_effects=True, vmem_limit_bytes=48 << 20),
        name="step",
    )(clips, cot, gain, bias, weights)


def widen_kernel(slabs, sums, out, gain_out, bias_out, buffers, sems):
    units = UNITS // WIDEN
    rows = units * 16
    gain_out[...] = sums[0:1]
    bias_out[...] = sums[1:2]

    def copy(i):
        return pltpu.make_async_copy(buffers.at[i % SLOTS], out.at[pl.ds(i * rows, rows)], sems.at[i % SLOTS])

    for i in range(WIDEN):
        if i >= SLOTS:
            copy(i - SLOTS).wait()
        for k in range(4):
            block = slabs[k, i * units : (i + 1) * units].reshape(rows, SLICE)
            buffers[i % SLOTS, :, k * SLICE : (k + 1) * SLICE] = block.astype(F32)
        copy(i).start()
    for i in range(WIDEN - SLOTS, WIDEN):
        copy(i).wait()


def widen(slabs, sums):
    vmem = pl.BlockSpec(memory_space=pltpu.VMEM)
    rows = UNITS // WIDEN * 16
    return pl.pallas_call(
        widen_kernel,
        out_shape=(
            jax.ShapeDtypeStruct((UNITS * 16, FULL), F32),
            jax.ShapeDtypeStruct((1, CH), F32),
            jax.ShapeDtypeStruct((1, CH), F32),
        ),
        in_specs=[vmem, vmem],
        out_specs=(pl.BlockSpec(memory_space=pl.ANY), vmem, vmem),
        scratch_shapes=[pltpu.VMEM((SLOTS, rows, FULL), F32), pltpu.SemaphoreType.DMA((SLOTS,))],
        compiler_params=pltpu.CompilerParams(vmem_limit_bytes=20 << 20),
        name="widen",
    )(slabs, sums)


def shards(clips, conv_weight, norm_gain, norm_bias, cotangent):
    slabs, sums = step(clips.reshape(4 * CH, 128), cotangent.reshape(4 * CH, 128), norm_gain, norm_bias, conv_weight[0])
    weight_grad, gain_grad, bias_grad = widen(slabs, sums)
    return weight_grad.reshape(1, 27, CH, FULL), gain_grad, bias_grad


def solution(mesh):
    in_specs = (
        P("dp", "chan", None, None),
        P("section", None, "chan", None),
        P("section", "chan"),
        P("section", "chan"),
        P("dp", "chan", None, None),
    )
    out_specs = (P("section", None, "chan", None), P("section", "chan"), P("section", "chan"))
    return jax.shard_map(shards, mesh=mesh, in_specs=in_specs, out_specs=out_specs, check_vma=False)
```
